32 devices in a mesh: ctx: 16 (over z, x, core), tp: 2 (over y).
Axes of the slice: x: 2, y: 2, z: 4, core: 2. Of those that a mesh axis runs over, the one named last changes fastest.
Arguments:
- query: bfloat16 [2048, 4096], P('ctx', 'tp'), as said below
- key_proj: bfloat16 [2048, 4096], P('ctx', 'tp'), may hold values from -6 to 6
- value_proj: bfloat16 [2048, 4096], P('ctx', 'tp'), may hold values from -6 to 6
- filter_taps: bfloat16 [2048, 4096], P('ctx', 'tp'), may hold values from -6 to 6
- grad_out: bfloat16 [2048, 4096], P('ctx', 'tp'), may hold values from -6 to 6
Outputs:
- mixer_out: bfloat16 [2048, 4096], P('ctx', 'tp')
- dquery: bfloat16 [2048, 4096], P('ctx', 'tp')
- dkey: bfloat16 [2048, 4096], P('ctx', 'tp')
- dvalue: bfloat16 [2048, 4096], P('ctx', 'tp')
- dtaps: bfloat16 [2048, 4096], P('ctx', 'tp')
The draws below stay inside these ranges and needn't reach their ends.
Inputs may be any that keep to these rules, and one draw needn't show every extreme that they name: Entries of query are real values of either sign.
All inputs are finite; a program needn't handle non-finite values.
Results may differ from the reference program's by a relative error of at most 0.0085.
Values may be sent and summed in bfloat16 or wider, within the bound.
No kernel may reach another device: no remote copies, remote signals or barrier semaphores. Data moves between devices by JAX's collectives and lax.ppermute only.
A program may use at most 64 MiB of HBM per device.

```python
import math
import jax
import jax.numpy as jnp
from jax import lax

W = 4096
L = 2048


def draw_query(key, part):
    first_key, second_key = jax.random.split(key, 2)
    channel_pos = jnp.arange(W, dtype=jnp.float32) / W
    spread = jnp.exp(jax.random.uniform(second_key, (W,), jnp.float32, 0.0, math.log(10.0)))
    column_scale = spread * 3.0 ** channel_pos
    base = jnp.clip(jax.random.normal(first_key, (L, W), jnp.float32), -6.0, 6.0)
    return (0.3 * base * column_scale[None, :]).astype(jnp.bfloat16)


def steps_of(stream_key, shape, pieces, low, top_value):
    loudness, own = 1.0, jax.random.fold_in(stream_key, 6)
    for axis_at, blocks in pieces:
        heights = jnp.exp(jax.random.uniform(jax.random.fold_in(own, axis_at), (blocks,), jnp.float32, low / len(pieces), top_value / len(pieces)))
        loudness = loudness * jnp.repeat(heights, shape[axis_at] // blocks).reshape([-1 if axis == axis_at else 1 for axis in range(len(shape))])
    return loudness


def normal_values(key, extent, scale, most, cuts=(), held_as=jnp.bfloat16):
    array = jax.random.normal(key, extent, jnp.float32) * scale
    if len(cuts) > 0:
        array = steps_of(key, extent, cuts, -0.22, 0.18) * array
    return jnp.clip(array, min=-most, max=most).astype(held_as)


def setup_inputs(seed: int = 0) -> dict:
    streams_of = jax.random.split(jax.random.key(seed), 6)
    query = draw_query(jax.random.fold_in(streams_of[5], 71), 0)
    key_proj = normal_values(streams_of[1], (L, W), 1.0, 6.0, ((0, 16), (1, 2)))
    value_proj = normal_values(streams_of[2], (L, W), 1.0, 6.0, ((0, 16), (1, 2)))
    filter_taps = normal_values(streams_of[3], (L, W), 1.0, 6.0, ((0, 16), (1, 2)))
    grad_out = normal_values(streams_of[4], (L, W), 1.0, 6.0, ((0, 16), (1, 2)))
    return dict(query=query, key_proj=key_proj, value_proj=value_proj, filter_taps=filter_taps, grad_out=grad_out)


def column_groups(matrix):
    length, width = matrix.shape
    group_size = min(width, 512)
    return matrix.reshape(length, width // group_size, group_size).transpose(1, 0, 2)

def joined(groups):
    group_count, length, group_size = groups.shape
    return groups.transpose(1, 0, 2).reshape(length, group_count * group_size)

def causal_filter(operands):
    taps, signal = operands
    length = taps.shape[0]
    spectrum = jnp.fft.rfft(taps, n=2 * length, axis=0) * jnp.fft.rfft(signal, n=2 * length, axis=0)
    return jnp.fft.irfft(spectrum, n=2 * length, axis=0)[:length]

def correlation(operands):
    later, earlier = operands
    length = later.shape[0]
    spectrum = jnp.fft.rfft(later, n=2 * length, axis=0) * jnp.conj(jnp.fft.rfft(earlier, n=2 * length, axis=0))
    return jnp.fft.irfft(spectrum, n=2 * length, axis=0)[:length]

def reference(query, key_proj, value_proj, filter_taps, grad_out):
    filter_scale = 1.0 / math.sqrt(L)
    key_float = key_proj.astype(jnp.float32)
    value_float = value_proj.astype(jnp.float32)
    mixed_rows = lax.optimization_barrier((key_float * value_float).astype(jnp.bfloat16))
    mixed_float = mixed_rows.astype(jnp.float32)
    taps_float = filter_taps.astype(jnp.float32)
    conv_full = filter_scale * joined(lax.map(causal_filter, (column_groups(taps_float), column_groups(mixed_float))))
    conv_rows = lax.optimization_barrier(conv_full.astype(jnp.bfloat16))
    conv_float = conv_rows.astype(jnp.float32)
    query_float = query.astype(jnp.float32)
    gated = query_float * conv_float
    inverse_rms = lax.rsqrt(lax.optimization_barrier(jnp.mean(gated * gated, axis=1)) + 1e-05)
    mixer_out = (gated * inverse_rms[:, None]).astype(jnp.bfloat16)
    upstream = grad_out.astype(jnp.float32)
    dots = lax.optimization_barrier(jnp.mean(upstream * gated, axis=1))
    dgated = inverse_rms[:, None] * upstream - (inverse_rms ** 3 * dots)[:, None] * gated
    dquery = (dgated * conv_float).astype(jnp.bfloat16)
    gconv = lax.optimization_barrier((dgated * query_float).astype(jnp.bfloat16))
    gconv_float = gconv.astype(jnp.float32)
    dmixed_full = filter_scale * joined(lax.map(correlation, (column_groups(gconv_float), column_groups(taps_float))))
    dmixed = lax.optimization_barrier(dmixed_full.astype(jnp.bfloat16))
    dtaps_full = filter_scale * joined(lax.map(correlation, (column_groups(gconv_float), column_groups(mixed_float))))
    dtaps = dtaps_full.astype(jnp.bfloat16)
    dmixed_float = dmixed.astype(jnp.float32)
    dkey = (dmixed_float * value_float).astype(jnp.bfloat16)
    dvalue = (dmixed_float * key_float).astype(jnp.bfloat16)
    return (mixer_out, dquery, dkey, dvalue, dtaps)
```

```python
import math

import jax
import jax.numpy as jnp
import numpy as np
from jax import lax
from jax.experimental import pallas as pl
from jax.experimental.pallas import tpu as pltpu
from jax.sharding import PartitionSpec as P

precise = lax.Precision.HIGHEST


def dft_tables(size_count):
    index = jnp.arange(size_count, dtype=jnp.int32)
    angle = (
        2.0
        * math.pi
        / size_count
        * (index[:, None] * index[None, :] % size_count).astype(jnp.float32)
    )
    return (jnp.cos(angle), jnp.sin(angle))


def twiddles(row_count, col_count):
    total = row_count * col_count
    row_index = jnp.arange(row_count, dtype=jnp.int32)
    col_index = jnp.arange(col_count, dtype=jnp.int32)
    angle = (
        2.0
        * math.pi
        / total
        * (row_index[:, None] * col_index[None, :] % total).astype(jnp.float32)
    )
    return (jnp.cos(angle), jnp.sin(angle))


def left_apply(table, blocks):
    return jnp.einsum("ka,cab->ckb", table, blocks, precision=precise)


def right_apply(blocks, table):
    return jnp.einsum("cka,ab->ckb", blocks, table, precision=precise)


def spectrum(signal):
    channels, length = signal.shape
    total = 2 * length
    row_count = 128
    col_count = total // row_count
    padded = jnp.concatenate(
        [signal.astype(jnp.float32), jnp.zeros((channels, length), jnp.float32)], axis=1
    )
    padded = padded.reshape(channels, row_count, col_count)
    cos_rows, sin_rows = dft_tables(row_count)
    cos_cols, sin_cols = dft_tables(col_count)
    cos_twist, sin_twist = twiddles(row_count, col_count)
    first_real = left_apply(cos_rows, padded)
    first_imag = -left_apply(sin_rows, padded)
    turned_real = first_real * cos_twist + first_imag * sin_twist
    turned_imag = first_imag * cos_twist - first_real * sin_twist
    spec_real = right_apply(turned_real, cos_cols) + right_apply(turned_imag, sin_cols)
    spec_imag = right_apply(turned_imag, cos_cols) - right_apply(turned_real, sin_cols)
    return (spec_real, spec_imag)


def signal_of(spec_real, spec_imag, length):
    channels, row_count, col_count = spec_real.shape
    total = row_count * col_count
    cos_rows, sin_rows = dft_tables(row_count)
    cos_cols, sin_cols = dft_tables(col_count)
    cos_twist, sin_twist = twiddles(row_count, col_count)
    back_real = right_apply(spec_real, cos_cols) - right_apply(spec_imag, sin_cols)
    back_imag = right_apply(spec_imag, cos_cols) + right_apply(spec_real, sin_cols)
    turned_real = back_real * cos_twist - back_imag * sin_twist
    turned_imag = back_imag * cos_twist + back_real * sin_twist
    values = left_apply(cos_rows, turned_real) - left_apply(sin_rows, turned_imag)
    return values.reshape(channels, total)[:, :length] / total


def times_plain(left_real, left_imag, right_real, right_imag):
    return (
        left_real * right_real - left_imag * right_imag,
        left_real * right_imag + left_imag * right_real,
    )


def times_conj(left_real, left_imag, right_real, right_imag):
    return (
        left_real * right_real + left_imag * right_imag,
        left_imag * right_real - left_real * right_imag,
    )


def channel_total(values):
    return lax.psum(values, "tp")


def per_device_plain(query, key_proj, value_proj, filter_taps, grad_out):
    length = query.shape[0] * lax.axis_size("ctx")
    width = query.shape[1] * lax.axis_size("tp")
    filter_scale = 1.0 / math.sqrt(length)
    mixed_rows = (key_proj.astype(jnp.float32) * value_proj.astype(jnp.float32)).astype(
        jnp.bfloat16
    )
    mixed_cols, taps_cols = (
        lax.all_to_all(mixed_rows.T, "ctx", split_axis=0, concat_axis=1, tiled=True),
        lax.all_to_all(filter_taps.T, "ctx", split_axis=0, concat_axis=1, tiled=True),
    )
    taps_real, taps_imag = spectrum(taps_cols)
    mixed_real, mixed_imag = spectrum(mixed_cols)
    conv_real, conv_imag = times_plain(mixed_real, mixed_imag, taps_real, taps_imag)
    conv_cols = (filter_scale * signal_of(conv_real, conv_imag, length)).astype(jnp.bfloat16)
    conv_rows = lax.all_to_all(conv_cols, "ctx", split_axis=1, concat_axis=0, tiled=True).T
    conv_float = conv_rows.astype(jnp.float32)
    query_float = query.astype(jnp.float32)
    gated = query_float * conv_float
    upstream = grad_out.astype(jnp.float32)
    square_sum = channel_total(jnp.sum(gated * gated, axis=1))
    inverse_rms = lax.rsqrt(square_sum / width + 1e-05)
    mixer_out = (gated * inverse_rms[:, None]).astype(jnp.bfloat16)
    dots = channel_total(jnp.sum(upstream * gated, axis=1)) / width
    dgated = inverse_rms[:, None] * upstream - (inverse_rms**3 * dots)[:, None] * gated
    dquery = (dgated * conv_float).astype(jnp.bfloat16)
    gconv = (dgated * query_float).astype(jnp.bfloat16)
    grad_cols = lax.all_to_all(gconv.T, "ctx", split_axis=0, concat_axis=1, tiled=True)
    grad_real, grad_imag = spectrum(grad_cols)
    back_real, back_imag = times_conj(grad_real, grad_imag, taps_real, taps_imag)
    dmixed_cols = (filter_scale * signal_of(back_real, back_imag, length)).astype(jnp.bfloat16)
    tap_real, tap_imag = times_conj(grad_real, grad_imag, mixed_real, mixed_imag)
    dtaps_cols = (filter_scale * signal_of(tap_real, tap_imag, length)).astype(jnp.bfloat16)
    dmixed_back, dtaps_back = (
        lax.all_to_all(dmixed_cols, "ctx", split_axis=1, concat_axis=0, tiled=True),
        lax.all_to_all(dtaps_cols, "ctx", split_axis=1, concat_axis=0, tiled=True),
    )
    dmixed_float = dmixed_back.T.astype(jnp.float32)
    dkey = (dmixed_float * value_proj.astype(jnp.float32)).astype(jnp.bfloat16)
    dvalue = (dmixed_float * key_proj.astype(jnp.float32)).astype(jnp.bfloat16)
    dtaps = dtaps_back.T
    return (mixer_out, dquery, dkey, dvalue, dtaps)


LANES = 128
ROWS = 16


def odd_tables(block):
    order = np.concatenate([np.arange(0, block, 2), np.arange(1, block, 2)])
    angle = np.pi * np.outer(2 * order + 1, np.arange(block)) / (2 * block)
    forward = np.concatenate([np.cos(angle), -np.sin(angle)], axis=0)
    high = forward.astype(jnp.bfloat16)
    low = (forward - high.astype(np.float64)).astype(jnp.bfloat16)
    return high, low


def params(flops, moved):
    return dict(
        compiler_params=pltpu.CompilerParams(vmem_limit_bytes=24 * 2**20),
        cost_estimate=pl.CostEstimate(flops=flops, bytes_accessed=moved, transcendentals=0),
    )


def whole(count):
    return [pl.BlockSpec(memory_space=pltpu.VMEM)] * count


def pack_kernel(key_ref, value_ref, taps_ref, out_ref):
    tokens = key_ref.shape[0]
    for piece in range(out_ref.shape[0]):
        cols = slice(piece * LANES, (piece + 1) * LANES)
        key = key_ref[:, cols].astype(jnp.float32)
        value = value_ref[:, cols].astype(jnp.float32)
        out_ref[piece, :tokens, :] = (key * value).astype(jnp.bfloat16)
        out_ref[piece, tokens:, :] = taps_ref[:, cols]


def pack(key_proj, value_proj, taps):
    tokens, width = key_proj.shape
    pieces = width // LANES
    step = 4 if pieces % 4 == 0 else pieces
    wide = pl.BlockSpec((tokens, step * LANES), lambda i: (0, i))
    return pl.pallas_call(
        pack_kernel,
        grid=(pieces // step,),
        in_specs=[wide] * 3,
        out_specs=pl.BlockSpec((step, 2 * tokens, LANES), lambda i: (i, 0, 0)),
        out_shape=jax.ShapeDtypeStruct((pieces, 2 * tokens, LANES), jnp.bfloat16),
        name="pack",
        **params(tokens * width, 10 * tokens * width),
    )(key_proj, value_proj, taps)


def block_columns(ref, offset, tokens, block):
    per = block // tokens
    blocks = []
    for b in range(ref.shape[0] // per):
        parts = [ref[b * per + p, offset : offset + tokens, :] for p in range(per)]
        blocks.append(jnp.concatenate(parts, axis=0))
    return jnp.concatenate(blocks, axis=1)


def to_spectrum(high_ref, low_ref, columns):
    return jnp.dot(high_ref[...], columns, preferred_element_type=jnp.float32) + jnp.dot(
        low_ref[...], columns, preferred_element_type=jnp.float32
    )


def store_signal(high_ref, low_ref, spec_ref, out_ref, offset, tokens, scale):
    block = high_ref.shape[0]
    per = block // tokens
    spec = spec_ref[...]
    signal = jnp.dot(high_ref[...], spec, preferred_element_type=jnp.float32) + jnp.dot(
        low_ref[...], spec, preferred_element_type=jnp.float32
    )
    rounded = (signal * scale).astype(jnp.bfloat16)
    for b in range(out_ref.shape[0] // per):
        for p in range(per):
            out_ref[b * per + p, offset : offset + tokens, :] = rounded[
                p * tokens : (p + 1) * tokens, b * LANES : (b + 1) * LANES
            ]


def each_tile(block, body):
    half = block // 2
    for sign, base in ((1.0, 0), (-1.0, half)):

        def step(i, carry, sign=sign, base=base):
            body(pl.multiple_of(base + i * ROWS, ROWS), sign)
            return carry

        lax.fori_loop(0, half // ROWS, step, 0)


def tile_of(ref, row, b, block):
    cols = slice(b * LANES, (b + 1) * LANES)
    return (ref[pl.ds(row, ROWS), cols], ref[pl.ds(row + block, ROWS), cols])


def put_tile(ref, row, b, block, real, imag):
    cols = slice(b * LANES, (b + 1) * LANES)
    ref[pl.ds(row, ROWS), cols] = real.astype(ref.dtype)
    ref[pl.ds(row + block, ROWS), cols] = imag.astype(ref.dtype)


def forward_kernel(scale, in_ref, fh_ref, fl_ref, bh_ref, bl_ref, out_ref, mix_ref, tap_ref, acc_ref):
    block = fh_ref.shape[1]
    tokens = out_ref.shape[1]
    count = mix_ref.shape[1] // LANES
    mix_ref[...] = to_spectrum(fh_ref, fl_ref, block_columns(in_ref, 0, tokens, block))
    tap_ref[...] = to_spectrum(fh_ref, fl_ref, block_columns(in_ref, tokens, tokens, block))

    def body(row, sign):
        taps = [tile_of(tap_ref, row, b, block) for b in range(count)]
        before = None
        for d in range(count):
            real = imag = None
            for j in range(d + 1):
                mr, mi = tile_of(mix_ref, row, j, block)
                tr, ti = taps[d - j]
                re = mr * tr - mi * ti
                im = mr * ti + mi * tr
                real = re if real is None else real + re
                imag = im if imag is None else imag + im
            if before is None:
                put_tile(acc_ref, row, d, block, real, imag)
            elif sign > 0:
                put_tile(acc_ref, row, d, block, real - before[1], imag + before[0])
            else:
                put_tile(acc_ref, row, d, block, real + before[1], imag - before[0])
            before = (real, imag)

    each_tile(block, body)
    store_signal(bh_ref, bl_ref, acc_ref, out_ref, 0, tokens, scale)


def backward_kernel(
    scale, in_ref, mix_ref, tap_ref, fh_ref, fl_ref, bh_ref, bl_ref, out_ref, grad_ref, acc_ref
):
    block = fh_ref.shape[1]
    tokens = in_ref.shape[1]
    count = mix_ref.shape[1] // LANES
    grad_ref[...] = to_spectrum(fh_ref, fl_ref, block_columns(in_ref, 0, tokens, block))
    for which, other_ref in enumerate((tap_ref, mix_ref)):

        def body(row, sign, other_ref=other_ref):
            others = [tile_of(other_ref, row, b, block) for b in range(count)]
            after = None
            for d in reversed(range(count)):
                real = imag = None
                for k in range(count - d):
                    gr, gi = tile_of(grad_ref, row, d + k, block)
                    ar, ai = others[k]
                    re = gr * ar + gi * ai
                    im = gi * ar - gr * ai
                    real = re if real is None else real + re
                    imag = im if imag is None else imag + im
                if after is None:
                    put_tile(acc_ref, row, d, block, real, imag)
                elif sign > 0:
                    put_tile(acc_ref, row, d, block, real + after[1], imag - after[0])
                else:
                    put_tile(acc_ref, row, d, block, real - after[1], imag + after[0])
                after = (real, imag)

        each_tile(block, body)
        store_signal(bh_ref, bl_ref, acc_ref, out_ref, which * tokens, tokens, scale)


def convolve(received, tables, scale):
    pieces, rows, _ = received.shape
    tokens = rows // 2
    fh, fl, bh, bl = tables
    freq, block = fh.shape
    wide = pieces * tokens // block * LANES
    spectrum_shape = jax.ShapeDtypeStruct((freq, wide), jnp.float32)

    def kernel(*refs):
        forward_kernel(scale, *refs)

    return pl.pallas_call(
        kernel,
        in_specs=whole(5),
        out_specs=whole(3),
        out_shape=(
            jax.ShapeDtypeStruct((pieces, tokens, LANES), jnp.bfloat16),
            spectrum_shape,
            spectrum_shape,
        ),
        scratch_shapes=[pltpu.VMEM((freq, wide), jnp.bfloat16)],
        name="forward",
        **params(12 * freq * block * wide, 8 * freq * wide),
    )(received, fh, fl, bh, bl)


def correlate(received, mix, tap, tables, scale):
    pieces, tokens, _ = received.shape
    fh, fl, bh, bl = tables
    freq, block = fh.shape
    wide = mix.shape[1]

    def kernel(*refs):
        backward_kernel(scale, *refs)

    return pl.pallas_call(
        kernel,
        in_specs=whole(7),
        out_specs=pl.BlockSpec(memory_space=pltpu.VMEM),
        out_shape=jax.ShapeDtypeStruct((pieces, 2 * tokens, LANES), jnp.bfloat16),
        scratch_shapes=[
            pltpu.VMEM((freq, wide), jnp.float32),
            pltpu.VMEM((freq, wide), jnp.bfloat16),
        ],
        name="backward",
        **params(12 * freq * block * wide, 8 * freq * wide),
    )(received, mix, tap, fh, fl, bh, bl)


def sums_kernel(query_ref, up_ref, conv_ref, out_ref):
    tokens = query_ref.shape[0]
    square = jnp.zeros((tokens, LANES), jnp.float32)
    cross = jnp.zeros((tokens, LANES), jnp.float32)
    for piece in range(conv_ref.shape[0]):
        cols = slice(piece * LANES, (piece + 1) * LANES)
        gated = query_ref[:, cols].astype(jnp.float32) * conv_ref[piece].astype(jnp.float32)
        square += gated * gated
        cross += up_ref[:, cols].astype(jnp.float32) * gated
    out_ref[0:1, :] = jnp.sum(square.T, axis=0, keepdims=True)
    out_ref[1:2, :] = jnp.sum(cross.T, axis=0, keepdims=True)


def token_sums(query, upstream, conv):
    tokens, width = query.shape
    return pl.pallas_call(
        sums_kernel,
        in_specs=whole(3),
        out_specs=pl.BlockSpec(memory_space=pltpu.VMEM),
        out_shape=jax.ShapeDtypeStruct((2, tokens), jnp.float32),
        name="sums",
        **params(5 * tokens * width, 6 * tokens * width),
    )(query, upstream, conv)


def norm_kernel(channels, sums_ref, query_ref, up_ref, conv_ref, mixer_ref, dquery_ref, grad_ref):
    tokens = query_ref.shape[0]
    mean = sums_ref[0:1, :] / channels
    dots = sums_ref[1:2, :] / channels
    inverse_row = lax.rsqrt(mean + 1e-05)
    slope_row = inverse_row * inverse_row * inverse_row * dots
    inverse = jnp.broadcast_to(inverse_row, (LANES, tokens)).T
    slope = jnp.broadcast_to(slope_row, (LANES, tokens)).T
    for piece in range(conv_ref.shape[0]):
        cols = slice(piece * LANES, (piece + 1) * LANES)
        conv = conv_ref[piece].astype(jnp.float32)
        query = query_ref[:, cols].astype(jnp.float32)
        gated = query * conv
        mixer_ref[:, cols] = (gated * inverse).astype(jnp.bfloat16)
        dgated = inverse * up_ref[:, cols].astype(jnp.float32) - slope * gated
        dquery_ref[:, cols] = (dgated * conv).astype(jnp.bfloat16)
        grad_ref[piece] = (dgated * query).astype(jnp.bfloat16)


def gate_norm(sums, query, upstream, conv, channels):
    tokens, width = query.shape

    def kernel(*refs):
        norm_kernel(channels, *refs)

    flat = jax.ShapeDtypeStruct((tokens, width), jnp.bfloat16)
    return pl.pallas_call(
        kernel,
        in_specs=whole(4),
        out_specs=whole(3),
        out_shape=(flat, flat, jax.ShapeDtypeStruct(conv.shape, jnp.bfloat16)),
        name="norm",
        **params(8 * tokens * width, 12 * tokens * width),
    )(sums, query, upstream, conv)


def unpack_kernel(back_ref, key_ref, value_ref, dkey_ref, dvalue_ref, dtaps_ref):
    tokens = key_ref.shape[0]
    for piece in range(back_ref.shape[0]):
        cols = slice(piece * LANES, (piece + 1) * LANES)
        dmixed = back_ref[piece, :tokens, :].astype(jnp.float32)
        dkey_ref[:, cols] = (dmixed * value_ref[:, cols].astype(jnp.float32)).astype(jnp.bfloat16)
        dvalue_ref[:, cols] = (dmixed * key_ref[:, cols].astype(jnp.float32)).astype(jnp.bfloat16)
        dtaps_ref[:, cols] = back_ref[piece, tokens:, :]


def unpack(back, key_proj, value_proj):
    tokens, width = key_proj.shape
    pieces = width // LANES
    step = 4 if pieces % 4 == 0 else pieces
    wide = pl.BlockSpec((tokens, step * LANES), lambda i: (0, i))
    flat = jax.ShapeDtypeStruct((tokens, width), jnp.bfloat16)
    return pl.pallas_call(
        unpack_kernel,
        grid=(pieces // step,),
        in_specs=[pl.BlockSpec((step, 2 * tokens, LANES), lambda i: (i, 0, 0)), wide, wide],
        out_specs=[wide] * 3,
        out_shape=(flat, flat, flat),
        name="unpack",
        **params(2 * tokens * width, 14 * tokens * width),
    )(back, key_proj, value_proj)


def exchange(pieces):
    return lax.all_to_all(pieces, "ctx", split_axis=0, concat_axis=0, tiled=True)


def per_device_kernels(query, key_proj, value_proj, filter_taps, grad_out):
    length = query.shape[0] * lax.axis_size("ctx")
    width = query.shape[1] * lax.axis_size("tp")
    block = 2 * query.shape[0]
    scale = 1.0 / (math.sqrt(length) * block)
    high, low = odd_tables(block)
    tables = tuple(jnp.asarray(t) for t in (high, low, high.T.copy(), low.T.copy()))
    received = exchange(pack(key_proj, value_proj, filter_taps))
    conv_cols, mix, tap = convolve(received, tables, scale)
    conv = exchange(conv_cols)
    sums = channel_total(token_sums(query, grad_out, conv))
    mixer_out, dquery, grad_rows = gate_norm(sums, query, grad_out, conv, width)
    back_cols = correlate(exchange(grad_rows), mix, tap, tables, scale)
    dkey, dvalue, dtaps = unpack(exchange(back_cols), key_proj, value_proj)
    return (mixer_out, dquery, dkey, dvalue, dtaps)


def per_device(query, key_proj, value_proj, filter_taps, grad_out):
    tokens, width = query.shape
    ring = lax.axis_size("ctx")
    if width == ring * LANES and tokens == LANES and ring % 2 == 0:
        return per_device_kernels(query, key_proj, value_proj, filter_taps, grad_out)
    return per_device_plain(query, key_proj, value_proj, filter_taps, grad_out)


def solution(mesh):
    in_specs = (P("ctx", "tp"), P("ctx", "tp"), P("ctx", "tp"), P("ctx", "tp"), P("ctx", "tp"))
    out_specs = (P("ctx", "tp"), P("ctx", "tp"), P("ctx", "tp"), P("ctx", "tp"), P("ctx", "tp"))
    return jax.shard_map(
        per_device, mesh=mesh, in_specs=in_specs, out_specs=out_specs, check_vma=False
    )
```

```python
import math

import jax
import jax.numpy as jnp
import numpy as np
from jax import lax
from jax.experimental import pallas as pl
from jax.experimental.pallas import tpu as pltpu
from jax.sharding import PartitionSpec as P

precise = lax.Precision.HIGHEST


def dft_tables(size_count):
    index = jnp.arange(size_count, dtype=jnp.int32)
    angle = (
        2.0
        * math.pi
        / size_count
        * (index[:, None] * index[None, :] % size_count).astype(jnp.float32)
    )
    return (jnp.cos(angle), jnp.sin(angle))


def twiddles(row_count, col_count):
    total = row_count * col_count
    row_index = jnp.arange(row_count, dtype=jnp.int32)
    col_index = jnp.arange(col_count, dtype=jnp.int32)
    angle = (
        2.0
        * math.pi
        / total
        * (row_index[:, None] * col_index[None, :] % total).astype(jnp.float32)
    )
    return (jnp.cos(angle), jnp.sin(angle))


def left_apply(table, blocks):
    return jnp.einsum("ka,cab->ckb", table, blocks, precision=precise)


def right_apply(blocks, table):
    return jnp.einsum("cka,ab->ckb", blocks, table, precision=precise)


def spectrum(signal):
    channels, length = signal.shape
    total = 2 * length
    row_count = 128
    col_count = total // row_count
    padded = jnp.concatenate(
        [signal.astype(jnp.float32), jnp.zeros((channels, length), jnp.float32)], axis=1
    )
    padded = padded.reshape(channels, row_count, col_count)
    cos_rows, sin_rows = dft_tables(row_count)
    cos_cols, sin_cols = dft_tables(col_count)
    cos_twist, sin_twist = twiddles(row_count, col_count)
    first_real = left_apply(cos_rows, padded)
    first_imag = -left_apply(sin_rows, padded)
    turned_real = first_real * cos_twist + first_imag * sin_twist
    turned_imag = first_imag * cos_twist - first_real * sin_twist
    spec_real = right_apply(turned_real, cos_cols) + right_apply(turned_imag, sin_cols)
    spec_imag = right_apply(turned_imag, cos_cols) - right_apply(turned_real, sin_cols)
    return (spec_real, spec_imag)


def signal_of(spec_real, spec_imag, length):
    channels, row_count, col_count = spec_real.shape
    total = row_count * col_count
    cos_rows, sin_rows = dft_tables(row_count)
    cos_cols, sin_cols = dft_tables(col_count)
    cos_twist, sin_twist = twiddles(row_count, col_count)
    back_real = right_apply(spec_real, cos_cols) - right_apply(spec_imag, sin_cols)
    back_imag = right_apply(spec_imag, cos_cols) + right_apply(spec_real, sin_cols)
    turned_real = back_real * cos_twist - back_imag * sin_twist
    turned_imag = back_imag * cos_twist + back_real * sin_twist
    values = left_apply(cos_rows, turned_real) - left_apply(sin_rows, turned_imag)
    return values.reshape(channels, total)[:, :length] / total


def times_plain(left_real, left_imag, right_real, right_imag):
    return (
        left_real * right_real - left_imag * right_imag,
        left_real * right_imag + left_imag * right_real,
    )


def times_conj(left_real, left_imag, right_real, right_imag):
    return (
        left_real * right_real + left_imag * right_imag,
        left_imag * right_real - left_real * right_imag,
    )


def channel_total(values):
    return lax.psum(values, "tp")


def per_device_plain(query, key_proj, value_proj, filter_taps, grad_out):
    length = query.shape[0] * lax.axis_size("ctx")
    width = query.shape[1] * lax.axis_size("tp")
    filter_scale = 1.0 / math.sqrt(length)
    mixed_rows = (key_proj.astype(jnp.float32) * value_proj.astype(jnp.float32)).astype(
        jnp.bfloat16
    )
    mixed_cols, taps_cols = (
        lax.all_to_all(mixed_rows.T, "ctx", split_axis=0, concat_axis=1, tiled=True),
        lax.all_to_all(filter_taps.T, "ctx", split_axis=0, concat_axis=1, tiled=True),
    )
    taps_real, taps_imag = spectrum(taps_cols)
    mixed_real, mixed_imag = spectrum(mixed_cols)
    conv_real, conv_imag = times_plain(mixed_real, mixed_imag, taps_real, taps_imag)
    conv_cols = (filter_scale * signal_of(conv_real, conv_imag, length)).astype(jnp.bfloat16)
    conv_rows = lax.all_to_all(conv_cols, "ctx", split_axis=1, concat_axis=0, tiled=True).T
    conv_float = conv_rows.astype(jnp.float32)
    query_float = query.astype(jnp.float32)
    gated = query_float * conv_float
    upstream = grad_out.astype(jnp.float32)
    square_sum = channel_total(jnp.sum(gated * gated, axis=1))
    inverse_rms = lax.rsqrt(square_sum / width + 1e-05)
    mixer_out = (gated * inverse_rms[:, None]).astype(jnp.bfloat16)
    dots = channel_total(jnp.sum(upstream * gated, axis=1)) / width
    dgated = inverse_rms[:, None] * upstream - (inverse_rms**3 * dots)[:, None] * gated
    dquery = (dgated * conv_float).astype(jnp.bfloat16)
    gconv = (dgated * query_float).astype(jnp.bfloat16)
    grad_cols = lax.all_to_all(gconv.T, "ctx", split_axis=0, concat_axis=1, tiled=True)
    grad_real, grad_imag = spectrum(grad_cols)
    back_real, back_imag = times_conj(grad_real, grad_imag, taps_real, taps_imag)
    dmixed_cols = (filter_scale * signal_of(back_real, back_imag, length)).astype(jnp.bfloat16)
    tap_real, tap_imag = times_conj(grad_real, grad_imag, mixed_real, mixed_imag)
    dtaps_cols = (filter_scale * signal_of(tap_real, tap_imag, length)).astype(jnp.bfloat16)
    dmixed_back, dtaps_back = (
        lax.all_to_all(dmixed_cols, "ctx", split_axis=1, concat_axis=0, tiled=True),
        lax.all_to_all(dtaps_cols, "ctx", split_axis=1, concat_axis=0, tiled=True),
    )
    dmixed_float = dmixed_back.T.astype(jnp.float32)
    dkey = (dmixed_float * value_proj.astype(jnp.float32)).astype(jnp.bfloat16)
    dvalue = (dmixed_float * key_proj.astype(jnp.float32)).astype(jnp.bfloat16)
    dtaps = dtaps_back.T
    return (mixer_out, dquery, dkey, dvalue, dtaps)


LANES = 128
ROWS = 16
STEPS = 4


def odd_tables(block):
    order = np.concatenate([np.arange(0, block, 2), np.arange(1, block, 2)])
    angle = np.pi * np.outer(2 * order + 1, np.arange(block)) / (2 * block)
    forward = np.concatenate([np.cos(angle), -np.sin(angle)], axis=0).astype(jnp.bfloat16)
    return jnp.asarray(forward), jnp.asarray(forward.T.copy())


def params(flops, moved, limit=16):
    return dict(
        compiler_params=pltpu.CompilerParams(vmem_limit_bytes=limit * 2**20),
        cost_estimate=pl.CostEstimate(flops=flops, bytes_accessed=moved, transcendentals=0),
    )


def whole(count):
    return [pl.BlockSpec(memory_space=pltpu.VMEM)] * count


def started(copies):
    for copy in copies:
        copy.start()
    return copies


def pack_kernel(
    key_hbm, value_hbm, taps_hbm, out_hbm, key_ref, value_ref, stage_ref, in_sems, tap_sems, out_sems
):
    pieces = stage_ref.shape[0]
    share = pieces // STEPS
    loads = []
    for i in range(STEPS):
        wide = slice(i * share * LANES, (i + 1) * share * LANES)
        group = [
            pltpu.make_async_copy(key_hbm.at[:, wide], key_ref.at[:, wide], in_sems.at[0, i]),
            pltpu.make_async_copy(value_hbm.at[:, wide], value_ref.at[:, wide], in_sems.at[1, i]),
        ]
        for piece in range(i * share, (i + 1) * share):
            col = slice(piece * LANES, (piece + 1) * LANES)
            group.append(
                pltpu.make_async_copy(taps_hbm.at[:, col], stage_ref.at[piece, 1], tap_sems.at[piece])
            )
        loads.append(started(group))
    stores = []
    for i, group in enumerate(loads):
        for copy in group:
            copy.wait()
        for piece in range(i * share, (i + 1) * share):
            col = slice(piece * LANES, (piece + 1) * LANES)
            product = key_ref[:, col].astype(jnp.float32) * value_ref[:, col].astype(jnp.float32)
            stage_ref[piece, 0] = product.astype(jnp.bfloat16)
        part = pl.ds(i * share, share)
        stores += started([pltpu.make_async_copy(stage_ref.at[part], out_hbm.at[part], out_sems.at[i])])
    for copy in stores:
        copy.wait()


def pack(key_proj, value_proj, taps):
    tokens, width = key_proj.shape
    pieces = width // LANES
    packed = pl.pallas_call(
        pack_kernel,
        in_specs=[pl.BlockSpec(memory_space=pltpu.HBM)] * 3,
        out_specs=pl.BlockSpec(memory_space=pltpu.HBM),
        out_shape=jax.ShapeDtypeStruct((pieces, 2, tokens, LANES), jnp.bfloat16),
        scratch_shapes=[
            pltpu.VMEM((tokens, width), jnp.bfloat16),
            pltpu.VMEM((tokens, width), jnp.bfloat16),
            pltpu.VMEM((pieces, 2, tokens, LANES), jnp.bfloat16),
            pltpu.SemaphoreType.DMA((2, STEPS)),
            pltpu.SemaphoreType.DMA((pieces,)),
            pltpu.SemaphoreType.DMA((STEPS,)),
        ],
        name="pack",
        **params(tokens * width, 10 * tokens * width, 63),
    )(key_proj, value_proj, taps)
    return packed.reshape(pieces, 2 * tokens, LANES)


def block_columns(ref, offset, tokens, block):
    per = block // tokens
    blocks = []
    for b in range(ref.shape[0] // per):
        parts = [ref[b * per + p, offset : offset + tokens, :] for p in range(per)]
        blocks.append(jnp.concatenate(parts, axis=0))
    return jnp.concatenate(blocks, axis=1)


def to_spectrum(table_ref, columns):
    return jnp.dot(table_ref[...], columns, preferred_element_type=jnp.float32)


def store_signal(back_ref, spec_ref, out_ref, offset, tokens, scale):
    per = back_ref.shape[0] // tokens
    signal = jnp.dot(back_ref[...], spec_ref[...], preferred_element_type=jnp.float32)
    rounded = (signal * scale).astype(jnp.bfloat16)
    for b in range(out_ref.shape[0] // per):
        for p in range(per):
            out_ref[b * per + p, offset : offset + tokens, :] = rounded[
                p * tokens : (p + 1) * tokens, b * LANES : (b + 1) * LANES
            ]


def each_tile(block, body):
    half = block // 2
    for sign, base in ((1.0, 0), (-1.0, half)):

        def step(i, carry, sign=sign, base=base):
            body(pl.multiple_of(base + i * ROWS, ROWS), sign)
            return carry

        lax.fori_loop(0, half // ROWS, step, 0)


def tile_of(ref, row, b, block):
    cols = slice(b * LANES, (b + 1) * LANES)
    return (ref[pl.ds(row, ROWS), cols], ref[pl.ds(row + block, ROWS), cols])


def put_tile(ref, row, b, block, real, imag):
    cols = slice(b * LANES, (b + 1) * LANES)
    ref[pl.ds(row, ROWS), cols] = real.astype(ref.dtype)
    ref[pl.ds(row + block, ROWS), cols] = imag.astype(ref.dtype)


def plus(total, term):
    return term if total is None else total + term


def forward_products(mix_ref, tap_ref, acc_ref, block):
    count = mix_ref.shape[1] // LANES

    def body(row, sign):
        taps = [tile_of(tap_ref, row, b, block) for b in range(count)]
        taps = [(r, i, r + i) for r, i in taps]
        mixes = [tile_of(mix_ref, row, b, block) for b in range(count)]
        mixes = [(r, i, r + i) for r, i in mixes]
        before = None
        for d in range(count):
            first = second = third = None
            for j in range(d + 1):
                mr, mi, ms = mixes[j]
                tr, ti, ts = taps[d - j]
                first = plus(first, mr * tr)
                second = plus(second, mi * ti)
                third = plus(third, ms * ts)
            real = first - second
            imag = third - first - second
            if before is None:
                put_tile(acc_ref, row, d, block, real, imag)
            elif sign > 0:
                put_tile(acc_ref, row, d, block, real - before[1], imag + before[0])
            else:
                put_tile(acc_ref, row, d, block, real + before[1], imag - before[0])
            before = (real, imag)

    each_tile(block, body)


def backward_products(grad_ref, other_ref, acc_ref, block):
    count = grad_ref.shape[1] // LANES

    def body(row, sign):
        others = [tile_of(other_ref, row, b, block) for b in range(count)]
        others = [(r, i, r - i) for r, i in others]
        grads = [tile_of(grad_ref, row, b, block) for b in range(count)]
        grads = [(r, i, r + i) for r, i in grads]
        after = None
        for d in reversed(range(count)):
            first = second = third = None
            for k in range(count - d):
                gr, gi, gs = grads[d + k]
                ar, ai, ad = others[k]
                first = plus(first, gr * ar)
                second = plus(second, gi * ai)
                third = plus(third, gs * ad)
            real = first + second
            imag = third - first + second
            if after is None:
                put_tile(acc_ref, row, d, block, real, imag)
            elif sign > 0:
                put_tile(acc_ref, row, d, block, real + after[1], imag - after[0])
            else:
                put_tile(acc_ref, row, d, block, real - after[1], imag + after[0])
            after = (real, imag)

    each_tile(block, body)


def forward_kernel(scale, in_ref, table_ref, back_ref, out_ref, mix_ref, tap_ref, acc_ref):
    block = table_ref.shape[1]
    tokens = out_ref.shape[1]
    mix_ref[...] = to_spectrum(table_ref, block_columns(in_ref, 0, tokens, block))
    tap_ref[...] = to_spectrum(table_ref, block_columns(in_ref, tokens, tokens, block))
    forward_products(mix_ref, tap_ref, acc_ref, block)
    store_signal(back_ref, acc_ref, out_ref, 0, tokens, scale)


def backward_kernel(
    scale, grad_in_ref, in_ref, table_ref, back_ref, out_ref, grad_ref, other_ref, acc_ref
):
    block = table_ref.shape[1]
    tokens = grad_in_ref.shape[1]
    grad_ref[...] = to_spectrum(table_ref, block_columns(grad_in_ref, 0, tokens, block))
    for which in range(2):
        columns = block_columns(in_ref, (1 - which) * tokens, tokens, block)
        other_ref[...] = to_spectrum(table_ref, columns)
        backward_products(grad_ref, other_ref, acc_ref, block)
        store_signal(back_ref, acc_ref, out_ref, which * tokens, tokens, scale)


def convolve(received, tables, scale):
    pieces, rows, _ = received.shape
    tokens = rows // 2
    freq, block = tables[0].shape
    wide = pieces * tokens // block * LANES

    def kernel(*refs):
        forward_kernel(scale, *refs)

    return pl.pallas_call(
        kernel,
        in_specs=whole(3),
        out_specs=pl.BlockSpec(memory_space=pltpu.VMEM),
        out_shape=jax.ShapeDtypeStruct((pieces, tokens, LANES), jnp.bfloat16),
        scratch_shapes=[
            pltpu.VMEM((freq, wide), jnp.float32),
            pltpu.VMEM((freq, wide), jnp.float32),
            pltpu.VMEM((freq, wide), jnp.bfloat16),
        ],
        name="forward",
        **params(6 * freq * block * wide, 8 * freq * wide),
    )(received, *tables)


def correlate(grads, received, tables, scale):
    pieces, tokens, _ = grads.shape
    freq, block = tables[0].shape
    wide = pieces * tokens // block * LANES

    def kernel(*refs):
        backward_kernel(scale, *refs)

    return pl.pallas_call(
        kernel,
        in_specs=whole(4),
        out_specs=pl.BlockSpec(memory_space=pltpu.VMEM),
        out_shape=jax.ShapeDtypeStruct((pieces, 2 * tokens, LANES), jnp.bfloat16),
        scratch_shapes=[
            pltpu.VMEM((freq, wide), jnp.float32),
            pltpu.VMEM((freq, wide), jnp.float32),
            pltpu.VMEM((freq, wide), jnp.bfloat16),
        ],
        name="backward",
        **params(10 * freq * block * wide, 8 * freq * wide),
    )(grads, received, *tables)


def sums_kernel(query_ref, up_ref, conv_ref, out_ref):
    tokens = query_ref.shape[0]
    square = jnp.zeros((tokens, LANES), jnp.float32)
    cross = jnp.zeros((tokens, LANES), jnp.float32)
    for piece in range(conv_ref.shape[0]):
        cols = slice(piece * LANES, (piece + 1) * LANES)
        gated = query_ref[:, cols].astype(jnp.float32) * conv_ref[piece].astype(jnp.float32)
        square += gated * gated
        cross += up_ref[:, cols].astype(jnp.float32) * gated
    out_ref[0:1, :] = jnp.sum(square.T, axis=0, keepdims=True)
    out_ref[1:2, :] = jnp.sum(cross.T, axis=0, keepdims=True)


def token_sums(query, upstream, conv):
    tokens, width = query.shape
    return pl.pallas_call(
        sums_kernel,
        in_specs=whole(3),
        out_specs=pl.BlockSpec(memory_space=pltpu.VMEM),
        out_shape=jax.ShapeDtypeStruct((2, tokens), jnp.float32),
        name="sums",
        **params(5 * tokens * width, 6 * tokens * width),
    )(query, upstream, conv)


def norm_kernel(
    channels,
    own_ref,
    other_ref,
    query_ref,
    up_ref,
    conv_ref,
    grad_ref,
    mixer_hbm,
    dquery_hbm,
    mixer_ref,
    dquery_ref,
    sems,
):
    tokens = query_ref.shape[0]
    sums = (own_ref[...] + other_ref[...]) / channels
    inverse_row = lax.rsqrt(sums[0:1, :] + 1e-05)
    slope_row = inverse_row * inverse_row * inverse_row * sums[1:2, :]
    inverses = jnp.broadcast_to(inverse_row, (LANES, tokens)).T
    slopes = jnp.broadcast_to(slope_row, (LANES, tokens)).T
    step = tokens // STEPS
    copies = []
    for i in range(STEPS):
        row = slice(i * step, (i + 1) * step)
        inverse, slope = inverses[row], slopes[row]
        for piece in range(conv_ref.shape[0]):
            cols = slice(piece * LANES, (piece + 1) * LANES)
            conv = conv_ref[piece, row, :].astype(jnp.float32)
            query = query_ref[row, cols].astype(jnp.float32)
            gated = query * conv
            mixer_ref[row, cols] = (gated * inverse).astype(jnp.bfloat16)
            dgated = inverse * up_ref[row, cols].astype(jnp.float32) - slope * gated
            dquery_ref[row, cols] = (dgated * conv).astype(jnp.bfloat16)
            grad_ref[piece, row, :] = (dgated * query).astype(jnp.bfloat16)
        copies += started(
            [
                pltpu.make_async_copy(source.at[row], target.at[row], sems.at[which, i])
                for which, (source, target) in enumerate(((mixer_ref, mixer_hbm), (dquery_ref, dquery_hbm)))
            ]
        )
    for copy in copies:
        copy.wait()


def gate_norm(own, other, query, upstream, conv, channels):
    tokens, width = query.shape

    def kernel(*refs):
        norm_kernel(channels, *refs)

    flat = jax.ShapeDtypeStruct((tokens, width), jnp.bfloat16)
    return pl.pallas_call(
        kernel,
        in_specs=whole(5),
        out_specs=[
            pl.BlockSpec(memory_space=pltpu.VMEM),
            pl.BlockSpec(memory_space=pltpu.HBM),
            pl.BlockSpec(memory_space=pltpu.HBM),
        ],
        out_shape=(jax.ShapeDtypeStruct(conv.shape, jnp.bfloat16), flat, flat),
        scratch_shapes=[
            pltpu.VMEM((tokens, width), jnp.bfloat16),
            pltpu.VMEM((tokens, width), jnp.bfloat16),
            pltpu.SemaphoreType.DMA((2, STEPS)),
        ],
        name="norm",
        **params(8 * tokens * width, 12 * tokens * width),
    )(own, other, query, upstream, conv)


def unpack_kernel(
    back_ref, key_ref, value_ref, dkey_hbm, dvalue_hbm, dtaps_hbm, dkey_ref, dvalue_ref, row_sems, tap_sems
):
    tokens = key_ref.shape[0]
    step = tokens // STEPS
    rows = [slice(i * step, (i + 1) * step) for i in range(STEPS)]
    cols = [slice(i * LANES, (i + 1) * LANES) for i in range(back_ref.shape[0])]
    copies = started(
        [
            pltpu.make_async_copy(
                back_ref.at[piece, pl.ds(tokens, tokens)], dtaps_hbm.at[:, col], tap_sems.at[piece]
            )
            for piece, col in enumerate(cols)
        ]
    )
    for i, row in enumerate(rows):
        for piece, col in enumerate(cols):
            dmixed = back_ref[piece, row, :].astype(jnp.float32)
            dkey_ref[row, col] = (dmixed * value_ref[row, col].astype(jnp.float32)).astype(jnp.bfloat16)
            dvalue_ref[row, col] = (dmixed * key_ref[row, col].astype(jnp.float32)).astype(jnp.bfloat16)
        copies += started(
            [
                pltpu.make_async_copy(source.at[row], target.at[row], row_sems.at[which, i])
                for which, (source, target) in enumerate(((dkey_ref, dkey_hbm), (dvalue_ref, dvalue_hbm)))
            ]
        )
    for copy in copies:
        copy.wait()


def unpack(back, key_proj, value_proj):
    tokens, width = key_proj.shape
    flat = jax.ShapeDtypeStruct((tokens, width), jnp.bfloat16)
    return pl.pallas_call(
        unpack_kernel,
        in_specs=whole(3),
        out_specs=[pl.BlockSpec(memory_space=pltpu.HBM)] * 3,
        out_shape=(flat, flat, flat),
        scratch_shapes=[
            pltpu.VMEM((tokens, width), jnp.bfloat16),
            pltpu.VMEM((tokens, width), jnp.bfloat16),
            pltpu.SemaphoreType.DMA((2, STEPS)),
            pltpu.SemaphoreType.DMA((width // LANES,)),
        ],
        name="unpack",
        **params(2 * tokens * width, 14 * tokens * width),
    )(back, key_proj, value_proj)


def exchange(pieces):
    return lax.all_to_all(pieces, "ctx", split_axis=0, concat_axis=0, tiled=True)


def per_device_kernels(query, key_proj, value_proj, filter_taps, grad_out):
    length = query.shape[0] * lax.axis_size("ctx")
    width = query.shape[1] * lax.axis_size("tp")
    block = 2 * query.shape[0]
    scale = 1.0 / (math.sqrt(length) * block)
    tables = odd_tables(block)
    received = exchange(pack(key_proj, value_proj, filter_taps))
    conv = exchange(convolve(received, tables, scale))
    own = token_sums(query, grad_out, conv)
    other = lax.ppermute(own, "tp", [(0, 1), (1, 0)])
    grads, mixer_out, dquery = gate_norm(own, other, query, grad_out, conv, width)
    back = exchange(correlate(exchange(grads), received, tables, scale))
    dkey, dvalue, dtaps = unpack(back, key_proj, value_proj)
    return (mixer_out, dquery, dkey, dvalue, dtaps)


def per_device(query, key_proj, value_proj, filter_taps, grad_out):
    tokens, width = query.shape
    ring = lax.axis_size("ctx")
    pairs = lax.axis_size("tp") == 2
    if pairs and width == ring * LANES and tokens == LANES and ring % 2 == 0:
        return per_device_kernels(query, key_proj, value_proj, filter_taps, grad_out)
    return per_device_plain(query, key_proj, value_proj, filter_taps, grad_out)


def solution(mesh):
    in_specs = (P("ctx", "tp"), P("ctx", "tp"), P("ctx", "tp"), P("ctx", "tp"), P("ctx", "tp"))
    out_specs = (P("ctx", "tp"), P("ctx", "tp"), P("ctx", "tp"), P("ctx", "tp"), P("ctx", "tp"))
    return jax.shard_map(
        per_device, mesh=mesh, in_specs=in_specs, out_specs=out_specs, check_vma=False
    )
```

```python
import math

import jax
import jax.numpy as jnp
import numpy as np
from jax import lax
from jax.experimental import pallas as pl
from jax.experimental.pallas import tpu as pltpu
from jax.sharding import PartitionSpec as P

precise = lax.Precision.HIGHEST


def dft_tables(size_count):
    index = jnp.arange(size_count, dtype=jnp.int32)
    angle = (
        2.0
        * math.pi
        / size_count
        * (index[:, None] * index[None, :] % size_count).astype(jnp.float32)
    )
    return (jnp.cos(angle), jnp.sin(angle))


def twiddles(row_count, col_count):
    total = row_count * col_count
    row_index = jnp.arange(row_count, dtype=jnp.int32)
    col_index = jnp.arange(col_count, dtype=jnp.int32)
    angle = (
        2.0
        * math.pi
        / total
        * (row_index[:, None] * col_index[None, :] % total).astype(jnp.float32)
    )
    return (jnp.cos(angle), jnp.sin(angle))


def left_apply(table, blocks):
    return jnp.einsum("ka,cab->ckb", table, blocks, precision=precise)


def right_apply(blocks, table):
    return jnp.einsum("cka,ab->ckb", blocks, table, precision=precise)


def spectrum(signal):
    channels, length = signal.shape
    total = 2 * length
    row_count = 128
    col_count = total // row_count
    padded = jnp.concatenate(
        [signal.astype(jnp.float32), jnp.zeros((channels, length), jnp.float32)], axis=1
    )
    padded = padded.reshape(channels, row_count, col_count)
    cos_rows, sin_rows = dft_tables(row_count)
    cos_cols, sin_cols = dft_tables(col_count)
    cos_twist, sin_twist = twiddles(row_count, col_count)
    first_real = left_apply(cos_rows, padded)
    first_imag = -left_apply(sin_rows, padded)
    turned_real = first_real * cos_twist + first_imag * sin_twist
    turned_imag = first_imag * cos_twist - first_real * sin_twist
    spec_real = right_apply(turned_real, cos_cols) + right_apply(turned_imag, sin_cols)
    spec_imag = right_apply(turned_imag, cos_cols) - right_apply(turned_real, sin_cols)
    return (spec_real, spec_imag)


def signal_of(spec_real, spec_imag, length):
    channels, row_count, col_count = spec_real.shape
    total = row_count * col_count
    cos_rows, sin_rows = dft_tables(row_count)
    cos_cols, sin_cols = dft_tables(col_count)
    cos_twist, sin_twist = twiddles(row_count, col_count)
    back_real = right_apply(spec_real, cos_cols) - right_apply(spec_imag, sin_cols)
    back_imag = right_apply(spec_imag, cos_cols) + right_apply(spec_real, sin_cols)
    turned_real = back_real * cos_twist - back_imag * sin_twist
    turned_imag = back_imag * cos_twist + back_real * sin_twist
    values = left_apply(cos_rows, turned_real) - left_apply(sin_rows, turned_imag)
    return values.reshape(channels, total)[:, :length] / total


def times_plain(left_real, left_imag, right_real, right_imag):
    return (
        left_real * right_real - left_imag * right_imag,
        left_real * right_imag + left_imag * right_real,
    )


def times_conj(left_real, left_imag, right_real, right_imag):
    return (
        left_real * right_real + left_imag * right_imag,
        left_imag * right_real - left_real * right_imag,
    )


def channel_total(values):
    return lax.psum(values, "tp")


def per_device_plain(query, key_proj, value_proj, filter_taps, grad_out):
    length = query.shape[0] * lax.axis_size("ctx")
    width = query.shape[1] * lax.axis_size("tp")
    filter_scale = 1.0 / math.sqrt(length)
    mixed_rows = (key_proj.astype(jnp.float32) * value_proj.astype(jnp.float32)).astype(
        jnp.bfloat16
    )
    mixed_cols, taps_cols = (
        lax.all_to_all(mixed_rows.T, "ctx", split_axis=0, concat_axis=1, tiled=True),
        lax.all_to_all(filter_taps.T, "ctx", split_axis=0, concat_axis=1, tiled=True),
    )
    taps_real, taps_imag = spectrum(taps_cols)
    mixed_real, mixed_imag = spectrum(mixed_cols)
    conv_real, conv_imag = times_plain(mixed_real, mixed_imag, taps_real, taps_imag)
    conv_cols = (filter_scale * signal_of(conv_real, conv_imag, length)).astype(jnp.bfloat16)
    conv_rows = lax.all_to_all(conv_cols, "ctx", split_axis=1, concat_axis=0, tiled=True).T
    conv_float = conv_rows.astype(jnp.float32)
    query_float = query.astype(jnp.float32)
    gated = query_float * conv_float
    upstream = grad_out.astype(jnp.float32)
    square_sum = channel_total(jnp.sum(gated * gated, axis=1))
    inverse_rms = lax.rsqrt(square_sum / width + 1e-05)
    mixer_out = (gated * inverse_rms[:, None]).astype(jnp.bfloat16)
    dots = channel_total(jnp.sum(upstream * gated, axis=1)) / width
    dgated = inverse_rms[:, None] * upstream - (inverse_rms**3 * dots)[:, None] * gated
    dquery = (dgated * conv_float).astype(jnp.bfloat16)
    gconv = (dgated * query_float).astype(jnp.bfloat16)
    grad_cols = lax.all_to_all(gconv.T, "ctx", split_axis=0, concat_axis=1, tiled=True)
    grad_real, grad_imag = spectrum(grad_cols)
    back_real, back_imag = times_conj(grad_real, grad_imag, taps_real, taps_imag)
    dmixed_cols = (filter_scale * signal_of(back_real, back_imag, length)).astype(jnp.bfloat16)
    tap_real, tap_imag = times_conj(grad_real, grad_imag, mixed_real, mixed_imag)
    dtaps_cols = (filter_scale * signal_of(tap_real, tap_imag, length)).astype(jnp.bfloat16)
    dmixed_back, dtaps_back = (
        lax.all_to_all(dmixed_cols, "ctx", split_axis=1, concat_axis=0, tiled=True),
        lax.all_to_all(dtaps_cols, "ctx", split_axis=1, concat_axis=0, tiled=True),
    )
    dmixed_float = dmixed_back.T.astype(jnp.float32)
    dkey = (dmixed_float * value_proj.astype(jnp.float32)).astype(jnp.bfloat16)
    dvalue = (dmixed_float * key_proj.astype(jnp.float32)).astype(jnp.bfloat16)
    dtaps = dtaps_back.T
    return (mixer_out, dquery, dkey, dvalue, dtaps)


LANES = 128
ROWS = 16
STEPS = 4
GROUPS = 4


def odd_tables(block):
    order = np.concatenate([np.arange(0, block, 2), np.arange(1, block, 2)])
    angle = np.pi * np.outer(2 * order + 1, np.arange(block)) / (2 * block)
    parts = np.stack([np.cos(angle), -np.sin(angle)]).reshape(2, GROUPS, block // GROUPS, block)
    forward = parts.transpose(1, 0, 2, 3).reshape(2 * block, block).astype(jnp.bfloat16)
    return jnp.asarray(forward), jnp.asarray(forward.T.copy())


def params(flops, moved, limit=16):
    return dict(
        compiler_params=pltpu.CompilerParams(vmem_limit_bytes=limit * 2**20),
        cost_estimate=pl.CostEstimate(flops=flops, bytes_accessed=moved, transcendentals=0),
    )


def whole(count):
    return [pl.BlockSpec(memory_space=pltpu.VMEM)] * count


def started(copies):
    for copy in copies:
        copy.start()
    return copies


def pack_kernel(
    key_hbm, value_hbm, taps_hbm, out_hbm, key_ref, value_ref, taps_ref, stage_ref, in_sems, out_sems
):
    pieces = stage_ref.shape[0]
    share = pieces // STEPS
    loads = []
    for i in range(STEPS):
        wide = slice(i * share * LANES, (i + 1) * share * LANES)
        group = [
            pltpu.make_async_copy(key_hbm.at[:, wide], key_ref.at[:, wide], in_sems.at[0, i]),
            pltpu.make_async_copy(value_hbm.at[:, wide], value_ref.at[:, wide], in_sems.at[1, i]),
        ]
        group.append(pltpu.make_async_copy(taps_hbm.at[:, wide], taps_ref.at[:, wide], in_sems.at[2, i]))
        loads.append(started(group))
    stores = []
    for i, group in enumerate(loads):
        for copy in group:
            copy.wait()
        for piece in range(i * share, (i + 1) * share):
            col = slice(piece * LANES, (piece + 1) * LANES)
            product = key_ref[:, col].astype(jnp.float32) * value_ref[:, col].astype(jnp.float32)
            stage_ref[piece, 0] = product.astype(jnp.bfloat16)
            stage_ref[piece, 1] = taps_ref[:, col]
        part = pl.ds(i * share, share)
        stores += started([pltpu.make_async_copy(stage_ref.at[part], out_hbm.at[part], out_sems.at[i])])
    for copy in stores:
        copy.wait()


def pack(key_proj, value_proj, taps):
    tokens, width = key_proj.shape
    pieces = width // LANES
    packed = pl.pallas_call(
        pack_kernel,
        in_specs=[pl.BlockSpec(memory_space=pltpu.HBM)] * 3,
        out_specs=pl.BlockSpec(memory_space=pltpu.HBM),
        out_shape=jax.ShapeDtypeStruct((pieces, 2, tokens, LANES), jnp.bfloat16),
        scratch_shapes=[
            pltpu.VMEM((tokens, width), jnp.bfloat16),
            pltpu.VMEM((tokens, width), jnp.bfloat16),
            pltpu.VMEM((tokens, width), jnp.bfloat16),
            pltpu.VMEM((pieces, 2, tokens, LANES), jnp.bfloat16),
            pltpu.SemaphoreType.DMA((3, STEPS)),
            pltpu.SemaphoreType.DMA((STEPS,)),
        ],
        name="pack",
        **params(tokens * width, 10 * tokens * width, 63),
    )(key_proj, value_proj, taps)
    return packed.reshape(pieces, 2 * tokens, LANES)


def transform(table_ref, spec_ref, group, in_ref, offset, tokens, tile):
    block = table_ref.shape[1]
    per = block // tokens
    blocks = []
    for b in range(2):
        parts = [
            in_ref[(2 * tile + b) * per + p, offset : offset + tokens, :] for p in range(per)
        ]
        blocks.append(jnp.concatenate(parts, axis=0))
    columns = jnp.concatenate(blocks, axis=1)
    size = spec_ref.shape[0]
    rows = table_ref[group * size : (group + 1) * size, :]
    lanes = pl.ds(tile * 2 * LANES, 2 * LANES)
    spec_ref[:, lanes] = jnp.dot(rows, columns, preferred_element_type=jnp.float32)


def restore(back_ref, acc_ref, out_ref, offset, tokens, scale, tile):
    per = back_ref.shape[0] // tokens
    lanes = slice(tile * 2 * LANES, (tile + 1) * 2 * LANES)
    signal = jnp.dot(back_ref[...], acc_ref[:, lanes], preferred_element_type=jnp.float32)
    rounded = (signal * scale).astype(jnp.bfloat16)
    for b in range(2):
        for p in range(per):
            out_ref[(2 * tile + b) * per + p, offset : offset + tokens, :] = rounded[
                p * tokens : (p + 1) * tokens, b * LANES : (b + 1) * LANES
            ]


def tile_of(ref, row, b):
    half = ref.shape[0] // 2
    cols = slice(b * LANES, (b + 1) * LANES)
    return (ref[pl.ds(row, ROWS), cols], ref[pl.ds(row + half, ROWS), cols])


def put_tile(ref, group, row, b, real, imag):
    size = ref.shape[0] // GROUPS
    cols = slice(b * LANES, (b + 1) * LANES)
    ref[pl.ds(group * size + row, ROWS), cols] = real.astype(ref.dtype)
    ref[pl.ds(group * size + size // 2 + row, ROWS), cols] = imag.astype(ref.dtype)


def plus(total, term):
    return term if total is None else total + term


def forward_products(mix_ref, tap_ref, acc_ref, group, row):
    count = mix_ref.shape[1] // LANES
    taps = [tile_of(tap_ref, row, b) for b in range(count)]
    taps = [(r, i, r + i) for r, i in taps]
    mixes = [tile_of(mix_ref, row, b) for b in range(count)]
    mixes = [(r, i, r + i) for r, i in mixes]
    before = None
    for d in range(count):
        first = second = third = None
        for j in range(d + 1):
            mr, mi, ms = mixes[j]
            tr, ti, ts = taps[d - j]
            first = plus(first, mr * tr)
            second = plus(second, mi * ti)
            third = plus(third, ms * ts)
        real = first - second
        imag = third - first - second
        if before is None:
            put_tile(acc_ref, group, row, d, real, imag)
        elif group < GROUPS // 2:
            put_tile(acc_ref, group, row, d, real - before[1], imag + before[0])
        else:
            put_tile(acc_ref, group, row, d, real + before[1], imag - before[0])
        before = (real, imag)


def backward_products(grad_ref, other_ref, acc_ref, group, row):
    count = grad_ref.shape[1] // LANES
    others = [tile_of(other_ref, row, b) for b in range(count)]
    others = [(r, i, r - i) for r, i in others]
    grads = [tile_of(grad_ref, row, b) for b in range(count)]
    grads = [(r, i, r + i) for r, i in grads]
    after = None
    for d in reversed(range(count)):
        first = second = third = None
        for k in range(count - d):
            gr, gi, gs = grads[d + k]
            ar, ai, ad = others[k]
            first = plus(first, gr * ar)
            second = plus(second, gi * ai)
            third = plus(third, gs * ad)
        real = first + second
        imag = third - first + second
        if after is None:
            put_tile(acc_ref, group, row, d, real, imag)
        elif group < GROUPS // 2:
            put_tile(acc_ref, group, row, d, real + after[1], imag - after[0])
        else:
            put_tile(acc_ref, group, row, d, real - after[1], imag + after[0])
        after = (real, imag)


def each_step(count, body):
    for i in range(count):
        body(i)


def forward_kernel(scale, in_ref, table_ref, back_ref, out_ref, acc_ref, *spectra):
    mixes, taps = spectra[:GROUPS], spectra[GROUPS:]
    tokens = out_ref.shape[1]
    tiles = acc_ref.shape[1] // (2 * LANES)

    def transforms(group, tile):
        transform(table_ref, mixes[group], group, in_ref, 0, tokens, tile)
        transform(table_ref, taps[group], group, in_ref, tokens, tokens, tile)

    for tile in range(tiles):
        transforms(0, tile)
    for group in range(GROUPS):

        def step(i, group=group):
            row = i * ROWS
            if group + 1 < GROUPS:
                transforms(group + 1, i)
            forward_products(mixes[group], taps[group], acc_ref, group, row)

        each_step(tiles, step)
    for tile in range(tiles):
        restore(back_ref, acc_ref, out_ref, 0, tokens, scale, tile)


def backward_kernel(scale, grad_in_ref, in_ref, table_ref, back_ref, out_ref, mixed_ref, dtaps_ref, *spectra):
    grads, taps, mixes = spectra[:GROUPS], spectra[GROUPS : 2 * GROUPS], spectra[2 * GROUPS :]
    tokens = grad_in_ref.shape[1]
    tiles = mixed_ref.shape[1] // (2 * LANES)

    def transforms(group, tile):
        transform(table_ref, grads[group], group, grad_in_ref, 0, tokens, tile)
        transform(table_ref, taps[group], group, in_ref, tokens, tokens, tile)

    for tile in range(tiles):
        transforms(0, tile)
    for group in range(GROUPS):

        def step(i, group=group):
            row = i * ROWS
            if group + 1 < GROUPS:
                transforms(group + 1, i)
            transform(table_ref, mixes[group], group, in_ref, 0, tokens, i)
            backward_products(grads[group], taps[group], mixed_ref, group, row)

        each_step(tiles, step)
    for group in range(GROUPS):

        def step(i, group=group):
            row = i * ROWS
            if i == 0:
                restore(back_ref, mixed_ref, out_ref, 0, tokens, scale, group)
            backward_products(grads[group], mixes[group], dtaps_ref, group, row)

        each_step(tiles, step)
    for tile in range(tiles):
        restore(back_ref, dtaps_ref, out_ref, tokens, tokens, scale, tile)


def convolve(received, tables, scale):
    pieces, rows, _ = received.shape
    tokens = rows // 2
    freq, block = tables[0].shape
    wide = pieces * tokens // block * LANES

    def kernel(*refs):
        forward_kernel(scale, *refs)

    return pl.pallas_call(
        kernel,
        in_specs=whole(3),
        out_specs=pl.BlockSpec(memory_space=pltpu.VMEM),
        out_shape=jax.ShapeDtypeStruct((pieces, tokens, LANES), jnp.bfloat16),
        scratch_shapes=[pltpu.VMEM((freq, wide), jnp.bfloat16)]
        + [pltpu.VMEM((freq // GROUPS, wide), jnp.float32)] * (2 * GROUPS),
        name="forward",
        **params(6 * freq * block * wide, 8 * freq * wide),
    )(received, *tables)


def correlate(grads, received, tables, scale):
    pieces, tokens, _ = grads.shape
    freq, block = tables[0].shape
    wide = pieces * tokens // block * LANES

    def kernel(*refs):
        backward_kernel(scale, *refs)

    return pl.pallas_call(
        kernel,
        in_specs=whole(4),
        out_specs=pl.BlockSpec(memory_space=pltpu.VMEM),
        out_shape=jax.ShapeDtypeStruct((pieces, 2 * tokens, LANES), jnp.bfloat16),
        scratch_shapes=[pltpu.VMEM((freq, wide), jnp.bfloat16)] * 2
        + [pltpu.VMEM((freq // GROUPS, wide), jnp.float32)] * (3 * GROUPS),
        name="backward",
        **params(10 * freq * block * wide, 8 * freq * wide),
    )(grads, received, *tables)


def sums_kernel(query_ref, up_ref, conv_ref, out_ref):
    tokens = query_ref.shape[0]
    square = jnp.zeros((tokens, LANES), jnp.float32)
    cross = jnp.zeros((tokens, LANES), jnp.float32)
    for piece in range(conv_ref.shape[0]):
        cols = slice(piece * LANES, (piece + 1) * LANES)
        gated = query_ref[:, cols].astype(jnp.float32) * conv_ref[piece].astype(jnp.float32)
        square += gated * gated
        cross += up_ref[:, cols].astype(jnp.float32) * gated
    out_ref[0:1, :] = jnp.sum(square.T, axis=0, keepdims=True)
    out_ref[1:2, :] = jnp.sum(cross.T, axis=0, keepdims=True)


def token_sums(query, upstream, conv):
    tokens, width = query.shape
    return pl.pallas_call(
        sums_kernel,
        in_specs=whole(3),
        out_specs=pl.BlockSpec(memory_space=pltpu.VMEM),
        out_shape=jax.ShapeDtypeStruct((2, tokens), jnp.float32),
        name="sums",
        **params(5 * tokens * width, 6 * tokens * width),
    )(query, upstream, conv)


def norm_kernel(
    channels,
    own_ref,
    other_ref,
    query_ref,
    up_ref,
    conv_ref,
    grad_ref,
    mixer_hbm,
    dquery_hbm,
    mixer_ref,
    dquery_ref,
    sems,
):
    tokens = query_ref.shape[0]
    sums = (own_ref[...] + other_ref[...]) / channels
    inverse_row = lax.rsqrt(sums[0:1, :] + 1e-05)
    slope_row = inverse_row * inverse_row * inverse_row * sums[1:2, :]
    inverses = jnp.broadcast_to(inverse_row, (LANES, tokens)).T
    slopes = jnp.broadcast_to(slope_row, (LANES, tokens)).T
    step = tokens // STEPS
    copies = []
    for i in range(STEPS):
        row = slice(i * step, (i + 1) * step)
        inverse, slope = inverses[row], slopes[row]
        for piece in range(conv_ref.shape[0]):
            cols = slice(piece * LANES, (piece + 1) * LANES)
            conv = conv_ref[piece, row, :].astype(jnp.float32)
            query = query_ref[row, cols].astype(jnp.float32)
            gated = query * conv
            mixer_ref[row, cols] = (gated * inverse).astype(jnp.bfloat16)
            dgated = inverse * up_ref[row, cols].astype(jnp.float32) - slope * gated
            dquery_ref[row, cols] = (dgated * conv).astype(jnp.bfloat16)
            grad_ref[piece, row, :] = (dgated * query).astype(jnp.bfloat16)
        copies += started(
            [
                pltpu.make_async_copy(source.at[row], target.at[row], sems.at[which, i])
                for which, (source, target) in enumerate(((mixer_ref, mixer_hbm), (dquery_ref, dquery_hbm)))
            ]
        )
    for copy in copies:
        copy.wait()


def gate_norm(own, other, query, upstream, conv, channels):
    tokens, width = query.shape

    def kernel(*refs):
        norm_kernel(channels, *refs)

    flat = jax.ShapeDtypeStruct((tokens, width), jnp.bfloat16)
    return pl.pallas_call(
        kernel,
        in_specs=whole(5),
        out_specs=[
            pl.BlockSpec(memory_space=pltpu.VMEM),
            pl.BlockSpec(memory_space=pltpu.HBM),
            pl.BlockSpec(memory_space=pltpu.HBM),
        ],
        out_shape=(jax.ShapeDtypeStruct(conv.shape, jnp.bfloat16), flat, flat),
        scratch_shapes=[
            pltpu.VMEM((tokens, width), jnp.bfloat16),
            pltpu.VMEM((tokens, width), jnp.bfloat16),
            pltpu.SemaphoreType.DMA((2, STEPS)),
        ],
        name="norm",
        **params(8 * tokens * width, 12 * tokens * width),
    )(own, other, query, upstream, conv)


def unpack_kernel(
    back_ref, key_ref, value_ref, dkey_hbm, dvalue_hbm, dtaps_hbm, dkey_ref, dvalue_ref, row_sems, tap_sems
):
    tokens = key_ref.shape[0]
    step = tokens // STEPS
    rows = [slice(i * step, (i + 1) * step) for i in range(STEPS)]
    cols = [slice(i * LANES, (i + 1) * LANES) for i in range(back_ref.shape[0])]
    copies = started(
        [
            pltpu.make_async_copy(
                back_ref.at[piece, pl.ds(tokens, tokens)], dtaps_hbm.at[:, col], tap_sems.at[piece]
            )
            for piece, col in enumerate(cols)
        ]
    )
    for i, row in enumerate(rows):
        for piece, col in enumerate(cols):
            dmixed = back_ref[piece, row, :].astype(jnp.float32)
            dkey_ref[row, col] = (dmixed * value_ref[row, col].astype(jnp.float32)).astype(jnp.bfloat16)
            dvalue_ref[row, col] = (dmixed * key_ref[row, col].astype(jnp.float32)).astype(jnp.bfloat16)
        copies += started(
            [
                pltpu.make_async_copy(source.at[row], target.at[row], row_sems.at[which, i])
                for which, (source, target) in enumerate(((dkey_ref, dkey_hbm), (dvalue_ref, dvalue_hbm)))
            ]
        )
    for copy in copies:
        copy.wait()


def unpack(back, key_proj, value_proj):
    tokens, width = key_proj.shape
    flat = jax.ShapeDtypeStruct((tokens, width), jnp.bfloat16)
    return pl.pallas_call(
        unpack_kernel,
        in_specs=whole(3),
        out_specs=[pl.BlockSpec(memory_space=pltpu.HBM)] * 3,
        out_shape=(flat, flat, flat),
        scratch_shapes=[
            pltpu.VMEM((tokens, width), jnp.bfloat16),
            pltpu.VMEM((tokens, width), jnp.bfloat16),
            pltpu.SemaphoreType.DMA((2, STEPS)),
            pltpu.SemaphoreType.DMA((width // LANES,)),
        ],
        name="unpack",
        **params(2 * tokens * width, 14 * tokens * width),
    )(back, key_proj, value_proj)


def exchange(pieces):
    return lax.all_to_all(pieces, "ctx", split_axis=0, concat_axis=0, tiled=True)


def per_device_kernels(query, key_proj, value_proj, filter_taps, grad_out):
    length = query.shape[0] * lax.axis_size("ctx")
    width = query.shape[1] * lax.axis_size("tp")
    block = 2 * query.shape[0]
    scale = 1.0 / (math.sqrt(length) * block)
    tables = odd_tables(block)
    received = exchange(pack(key_proj, value_proj, filter_taps))
    conv = exchange(convolve(received, tables, scale))
    own = token_sums(query, grad_out, conv)
    other = lax.ppermute(own, "tp", [(0, 1), (1, 0)])
    grads, mixer_out, dquery = gate_norm(own, other, query, grad_out, conv, width)
    back = exchange(correlate(exchange(grads), received, tables, scale))
    dkey, dvalue, dtaps = unpack(back, key_proj, value_proj)
    return (mixer_out, dquery, dkey, dvalue, dtaps)


def per_device(query, key_proj, value_proj, filter_taps, grad_out):
    tokens, width = query.shape
    ring = lax.axis_size("ctx")
    pairs = lax.axis_size("tp") == 2
    if pairs and width == ring * LANES and tokens == LANES and ring % 2 == 0:
        return per_device_kernels(query, key_proj, value_proj, filter_taps, grad_out)
    return per_device_plain(query, key_proj, value_proj, filter_taps, grad_out)


def solution(mesh):
    in_specs = (P("ctx", "tp"), P("ctx", "tp"), P("ctx", "tp"), P("ctx", "tp"), P("ctx", "tp"))
    out_specs = (P("ctx", "tp"), P("ctx", "tp"), P("ctx", "tp"), P("ctx", "tp"), P("ctx", "tp"))
    return jax.shard_map(
        per_device, mesh=mesh, in_specs=in_specs, out_specs=out_specs, check_vma=False
    )
```

```python
import math

import jax
import jax.numpy as jnp
import numpy as np
from jax import lax
from jax.experimental import pallas as pl
from jax.experimental.pallas import tpu as pltpu
from jax.sharding import PartitionSpec as P

precise = lax.Precision.HIGHEST


def dft_tables(size_count):
    index = jnp.arange(size_count, dtype=jnp.int32)
    angle = (
        2.0
        * math.pi
        / size_count
        * (index[:, None] * index[None, :] % size_count).astype(jnp.float32)
    )
    return (jnp.cos(angle), jnp.sin(angle))


def twiddles(row_count, col_count):
    total = row_count * col_count
    row_index = jnp.arange(row_count, dtype=jnp.int32)
    col_index = jnp.arange(col_count, dtype=jnp.int32)
    angle = (
        2.0
        * math.pi
        / total
        * (row_index[:, None] * col_index[None, :] % total).astype(jnp.float32)
    )
    return (jnp.cos(angle), jnp.sin(angle))


def left_apply(table, blocks):
    return jnp.einsum("ka,cab->ckb", table, blocks, precision=precise)


def right_apply(blocks, table):
    return jnp.einsum("cka,ab->ckb", blocks, table, precision=precise)


def spectrum(signal):
    channels, length = signal.shape
    total = 2 * length
    row_count = 128
    col_count = total // row_count
    padded = jnp.concatenate(
        [signal.astype(jnp.float32), jnp.zeros((channels, length), jnp.float32)], axis=1
    )
    padded = padded.reshape(channels, row_count, col_count)
    cos_rows, sin_rows = dft_tables(row_count)
    cos_cols, sin_cols = dft_tables(col_count)
    cos_twist, sin_twist = twiddles(row_count, col_count)
    first_real = left_apply(cos_rows, padded)
    first_imag = -left_apply(sin_rows, padded)
    turned_real = first_real * cos_twist + first_imag * sin_twist
    turned_imag = first_imag * cos_twist - first_real * sin_twist
    spec_real = right_apply(turned_real, cos_cols) + right_apply(turned_imag, sin_cols)
    spec_imag = right_apply(turned_imag, cos_cols) - right_apply(turned_real, sin_cols)
    return (spec_real, spec_imag)


def signal_of(spec_real, spec_imag, length):
    channels, row_count, col_count = spec_real.shape
    total = row_count * col_count
    cos_rows, sin_rows = dft_tables(row_count)
    cos_cols, sin_cols = dft_tables(col_count)
    cos_twist, sin_twist = twiddles(row_count, col_count)
    back_real = right_apply(spec_real, cos_cols) - right_apply(spec_imag, sin_cols)
    back_imag = right_apply(spec_imag, cos_cols) + right_apply(spec_real, sin_cols)
    turned_real = back_real * cos_twist - back_imag * sin_twist
    turned_imag = back_imag * cos_twist + back_real * sin_twist
    values = left_apply(cos_rows, turned_real) - left_apply(sin_rows, turned_imag)
    return values.reshape(channels, total)[:, :length] / total


def times_plain(left_real, left_imag, right_real, right_imag):
    return (
        left_real * right_real - left_imag * right_imag,
        left_real * right_imag + left_imag * right_real,
    )


def times_conj(left_real, left_imag, right_real, right_imag):
    return (
        left_real * right_real + left_imag * right_imag,
        left_imag * right_real - left_real * right_imag,
    )


def channel_total(values):
    return lax.psum(values, "tp")


def per_device_plain(query, key_proj, value_proj, filter_taps, grad_out):
    length = query.shape[0] * lax.axis_size("ctx")
    width = query.shape[1] * lax.axis_size("tp")
    filter_scale = 1.0 / math.sqrt(length)
    mixed_rows = (key_proj.astype(jnp.float32) * value_proj.astype(jnp.float32)).astype(
        jnp.bfloat16
    )
    mixed_cols, taps_cols = (
        lax.all_to_all(mixed_rows.T, "ctx", split_axis=0, concat_axis=1, tiled=True),
        lax.all_to_all(filter_taps.T, "ctx", split_axis=0, concat_axis=1, tiled=True),
    )
    taps_real, taps_imag = spectrum(taps_cols)
    mixed_real, mixed_imag = spectrum(mixed_cols)
    conv_real, conv_imag = times_plain(mixed_real, mixed_imag, taps_real, taps_imag)
    conv_cols = (filter_scale * signal_of(conv_real, conv_imag, length)).astype(jnp.bfloat16)
    conv_rows = lax.all_to_all(conv_cols, "ctx", split_axis=1, concat_axis=0, tiled=True).T
    conv_float = conv_rows.astype(jnp.float32)
    query_float = query.astype(jnp.float32)
    gated = query_float * conv_float
    upstream = grad_out.astype(jnp.float32)
    square_sum = channel_total(jnp.sum(gated * gated, axis=1))
    inverse_rms = lax.rsqrt(square_sum / width + 1e-05)
    mixer_out = (gated * inverse_rms[:, None]).astype(jnp.bfloat16)
    dots = channel_total(jnp.sum(upstream * gated, axis=1)) / width
    dgated = inverse_rms[:, None] * upstream - (inverse_rms**3 * dots)[:, None] * gated
    dquery = (dgated * conv_float).astype(jnp.bfloat16)
    gconv = (dgated * query_float).astype(jnp.bfloat16)
    grad_cols = lax.all_to_all(gconv.T, "ctx", split_axis=0, concat_axis=1, tiled=True)
    grad_real, grad_imag = spectrum(grad_cols)
    back_real, back_imag = times_conj(grad_real, grad_imag, taps_real, taps_imag)
    dmixed_cols = (filter_scale * signal_of(back_real, back_imag, length)).astype(jnp.bfloat16)
    tap_real, tap_imag = times_conj(grad_real, grad_imag, mixed_real, mixed_imag)
    dtaps_cols = (filter_scale * signal_of(tap_real, tap_imag, length)).astype(jnp.bfloat16)
    dmixed_back, dtaps_back = (
        lax.all_to_all(dmixed_cols, "ctx", split_axis=1, concat_axis=0, tiled=True),
        lax.all_to_all(dtaps_cols, "ctx", split_axis=1, concat_axis=0, tiled=True),
    )
    dmixed_float = dmixed_back.T.astype(jnp.float32)
    dkey = (dmixed_float * value_proj.astype(jnp.float32)).astype(jnp.bfloat16)
    dvalue = (dmixed_float * key_proj.astype(jnp.float32)).astype(jnp.bfloat16)
    dtaps = dtaps_back.T
    return (mixer_out, dquery, dkey, dvalue, dtaps)


LANES = 128
ROWS = 16
STEPS = 4
GROUPS = 4


def odd_tables(block):
    order = np.concatenate([np.arange(0, block, 2), np.arange(1, block, 2)])
    angle = np.pi * np.outer(2 * order + 1, np.arange(block)) / (2 * block)
    parts = np.stack([np.cos(angle), -np.sin(angle)]).reshape(2, GROUPS, block // GROUPS, block)
    forward = parts.transpose(1, 0, 2, 3).reshape(2 * block, block).astype(jnp.bfloat16)
    return jnp.asarray(forward), jnp.asarray(forward.T.copy())


def params(flops, moved, limit=16):
    return dict(
        compiler_params=pltpu.CompilerParams(vmem_limit_bytes=limit * 2**20),
        cost_estimate=pl.CostEstimate(flops=flops, bytes_accessed=moved, transcendentals=0),
    )


def whole(count):
    return [pl.BlockSpec(memory_space=pltpu.VMEM)] * count


def started(copies):
    for copy in copies:
        copy.start()
    return copies


def pack_kernel(
    key_hbm, value_hbm, taps_hbm, out_hbm, key_ref, value_ref, taps_ref, stage_ref, in_sems, out_sems
):
    pieces = stage_ref.shape[0]
    share = pieces // STEPS
    loads = []
    for i in range(STEPS):
        wide = slice(i * share * LANES, (i + 1) * share * LANES)
        group = [
            pltpu.make_async_copy(key_hbm.at[:, wide], key_ref.at[:, wide], in_sems.at[0, i]),
            pltpu.make_async_copy(value_hbm.at[:, wide], value_ref.at[:, wide], in_sems.at[1, i]),
        ]
        group.append(pltpu.make_async_copy(taps_hbm.at[:, wide], taps_ref.at[:, wide], in_sems.at[2, i]))
        loads.append(started(group))
    stores = []
    for i, group in enumerate(loads):
        for copy in group:
            copy.wait()
        for piece in range(i * share, (i + 1) * share):
            col = slice(piece * LANES, (piece + 1) * LANES)
            product = key_ref[:, col].astype(jnp.float32) * value_ref[:, col].astype(jnp.float32)
            stage_ref[piece, 0] = product.astype(jnp.bfloat16)
            stage_ref[piece, 1] = taps_ref[:, col]
        part = pl.ds(i * share, share)
        stores += started([pltpu.make_async_copy(stage_ref.at[part], out_hbm.at[part], out_sems.at[i])])
    for copy in stores:
        copy.wait()


def pack(key_proj, value_proj, taps):
    tokens, width = key_proj.shape
    pieces = width // LANES
    packed = pl.pallas_call(
        pack_kernel,
        in_specs=[pl.BlockSpec(memory_space=pltpu.HBM)] * 3,
        out_specs=pl.BlockSpec(memory_space=pltpu.HBM),
        out_shape=jax.ShapeDtypeStruct((pieces, 2, tokens, LANES), jnp.bfloat16),
        scratch_shapes=[
            pltpu.VMEM((tokens, width), jnp.bfloat16),
            pltpu.VMEM((tokens, width), jnp.bfloat16),
            pltpu.VMEM((tokens, width), jnp.bfloat16),
            pltpu.VMEM((pieces, 2, tokens, LANES), jnp.bfloat16),
            pltpu.SemaphoreType.DMA((3, STEPS)),
            pltpu.SemaphoreType.DMA((STEPS,)),
        ],
        name="pack",
        **params(tokens * width, 10 * tokens * width, 63),
    )(key_proj, value_proj, taps)
    return packed.reshape(pieces, 2 * tokens, LANES)


def transform(table_ref, spec_ref, group, in_ref, offset, tokens, tile):
    block = table_ref.shape[1]
    per = block // tokens
    blocks = []
    for b in range(2):
        parts = [
            in_ref[(2 * tile + b) * per + p, offset : offset + tokens, :] for p in range(per)
        ]
        blocks.append(jnp.concatenate(parts, axis=0))
    columns = jnp.concatenate(blocks, axis=1)
    size = spec_ref.shape[0]
    rows = table_ref[group * size : (group + 1) * size, :]
    lanes = pl.ds(tile * 2 * LANES, 2 * LANES)
    spec_ref[:, lanes] = jnp.dot(rows, columns, preferred_element_type=jnp.float32)


def restore(back_ref, acc_ref, out_ref, offset, tokens, scale, tile):
    per = back_ref.shape[0] // tokens
    lanes = slice(tile * 2 * LANES, (tile + 1) * 2 * LANES)
    signal = jnp.dot(back_ref[...], acc_ref[:, lanes], preferred_element_type=jnp.float32)
    rounded = (signal * scale).astype(jnp.bfloat16)
    for b in range(2):
        for p in range(per):
            out_ref[(2 * tile + b) * per + p, offset : offset + tokens, :] = rounded[
                p * tokens : (p + 1) * tokens, b * LANES : (b + 1) * LANES
            ]


def tile_of(ref, row, b):
    half = ref.shape[0] // 2
    cols = slice(b * LANES, (b + 1) * LANES)
    return (ref[pl.ds(row, ROWS), cols], ref[pl.ds(row + half, ROWS), cols])


def put_tile(ref, group, row, b, real, imag):
    size = ref.shape[0] // GROUPS
    cols = slice(b * LANES, (b + 1) * LANES)
    ref[pl.ds(group * size + row, ROWS), cols] = real.astype(ref.dtype)
    ref[pl.ds(group * size + size // 2 + row, ROWS), cols] = imag.astype(ref.dtype)


def plus(total, term):
    return term if total is None else total + term


def forward_products(mix_ref, tap_ref, acc_ref, group, row):
    count = mix_ref.shape[1] // LANES
    taps = [tile_of(tap_ref, row, b) for b in range(count)]
    taps = [(r, i, r + i) for r, i in taps]
    mixes = [tile_of(mix_ref, row, b) for b in range(count)]
    mixes = [(r, i, r + i) for r, i in mixes]
    before = None
    for d in range(count):
        first = second = third = None
        for j in range(d + 1):
            mr, mi, ms = mixes[j]
            tr, ti, ts = taps[d - j]
            first = plus(first, mr * tr)
            second = plus(second, mi * ti)
            third = plus(third, ms * ts)
        real = first - second
        imag = third - first - second
        if before is None:
            put_tile(acc_ref, group, row, d, real, imag)
        elif group < GROUPS // 2:
            put_tile(acc_ref, group, row, d, real - before[1], imag + before[0])
        else:
            put_tile(acc_ref, group, row, d, real + before[1], imag - before[0])
        before = (real, imag)


def backward_products(grad_ref, other_ref, acc_ref, group, row):
    count = grad_ref.shape[1] // LANES
    others = [tile_of(other_ref, row, b) for b in range(count)]
    others = [(r, i, r - i) for r, i in others]
    grads = [tile_of(grad_ref, row, b) for b in range(count)]
    grads = [(r, i, r + i) for r, i in grads]
    after = None
    for d in reversed(range(count)):
        first = second = third = None
        for k in range(count - d):
            gr, gi, gs = grads[d + k]
            ar, ai, ad = others[k]
            first = plus(first, gr * ar)
            second = plus(second, gi * ai)
            third = plus(third, gs * ad)
        real = first + second
        imag = third - first + second
        if after is None:
            put_tile(acc_ref, group, row, d, real, imag)
        elif group < GROUPS // 2:
            put_tile(acc_ref, group, row, d, real + after[1], imag - after[0])
        else:
            put_tile(acc_ref, group, row, d, real - after[1], imag + after[0])
        after = (real, imag)


def each_step(count, body):
    for i in range(count):
        body(i)


def forward_kernel(scale, in_ref, table_ref, back_ref, out_ref, acc_ref, *spectra):
    mixes, taps = spectra[:GROUPS], spectra[GROUPS:]
    tokens = out_ref.shape[1]
    tiles = acc_ref.shape[1] // (2 * LANES)

    def transforms(group, tile):
        transform(table_ref, mixes[group], group, in_ref, 0, tokens, tile)
        transform(table_ref, taps[group], group, in_ref, tokens, tokens, tile)

    for tile in range(tiles):
        transforms(0, tile)
    for group in range(GROUPS):

        def step(i, group=group):
            row = i * ROWS
            if group + 1 < GROUPS:
                transforms(group + 1, i)
            forward_products(mixes[group], taps[group], acc_ref, group, row)

        each_step(tiles, step)
    for tile in range(tiles):
        restore(back_ref, acc_ref, out_ref, 0, tokens, scale, tile)


def backward_kernel(
    scale, grad_in_ref, in_ref, table_ref, back_ref, out_hbm, out_ref, sems, mixed_ref, dtaps_ref, *spectra
):
    grads, taps, mixes = spectra[:GROUPS], spectra[GROUPS : 2 * GROUPS], spectra[2 * GROUPS :]
    tokens = grad_in_ref.shape[1]
    tiles = mixed_ref.shape[1] // (2 * LANES)

    copies = []

    def send(offset, which, tile):
        share = out_ref.shape[0] // tiles
        part = (pl.ds(tile * share, share), pl.ds(offset, tokens))
        copies.extend(
            started([pltpu.make_async_copy(out_ref.at[part], out_hbm.at[part], sems.at[which, tile])])
        )

    def transforms(group, tile):
        transform(table_ref, grads[group], group, grad_in_ref, 0, tokens, tile)
        transform(table_ref, taps[group], group, in_ref, tokens, tokens, tile)

    for tile in range(tiles):
        transforms(0, tile)
    for group in range(GROUPS):

        def step(i, group=group):
            row = i * ROWS
            if group + 1 < GROUPS:
                transforms(group + 1, i)
            transform(table_ref, mixes[group], group, in_ref, 0, tokens, i)
            backward_products(grads[group], taps[group], mixed_ref, group, row)

        each_step(tiles, step)
    for group in range(GROUPS):

        def step(i, group=group):
            row = i * ROWS
            if i == 0:
                restore(back_ref, mixed_ref, out_ref, 0, tokens, scale, group)
                send(0, 0, group)
            backward_products(grads[group], mixes[group], dtaps_ref, group, row)

        each_step(tiles, step)
    for tile in range(tiles):
        restore(back_ref, dtaps_ref, out_ref, tokens, tokens, scale, tile)
        send(tokens, 1, tile)
    for copy in copies:
        copy.wait()


def convolve(received, tables, scale):
    pieces, rows, _ = received.shape
    tokens = rows // 2
    freq, block = tables[0].shape
    wide = pieces * tokens // block * LANES

    def kernel(*refs):
        forward_kernel(scale, *refs)

    return pl.pallas_call(
        kernel,
        in_specs=whole(3),
        out_specs=pl.BlockSpec(memory_space=pltpu.VMEM),
        out_shape=jax.ShapeDtypeStruct((pieces, tokens, LANES), jnp.bfloat16),
        scratch_shapes=[pltpu.VMEM((freq, wide), jnp.bfloat16)]
        + [pltpu.VMEM((freq // GROUPS, wide), jnp.float32)] * (2 * GROUPS),
        name="forward",
        **params(6 * freq * block * wide, 8 * freq * wide),
    )(received, *tables)


def correlate(grads, received, tables, scale):
    pieces, tokens, _ = grads.shape
    freq, block = tables[0].shape
    wide = pieces * tokens // block * LANES

    def kernel(*refs):
        backward_kernel(scale, *refs)

    return pl.pallas_call(
        kernel,
        in_specs=whole(4),
        out_specs=pl.BlockSpec(memory_space=pltpu.HBM),
        out_shape=jax.ShapeDtypeStruct((pieces, 2 * tokens, LANES), jnp.bfloat16),
        scratch_shapes=[
            pltpu.VMEM((pieces, 2 * tokens, LANES), jnp.bfloat16),
            pltpu.SemaphoreType.DMA((2, GROUPS)),
        ]
        + [pltpu.VMEM((freq, wide), jnp.bfloat16)] * 2
        + [pltpu.VMEM((freq // GROUPS, wide), jnp.float32)] * (3 * GROUPS),
        name="backward",
        **params(10 * freq * block * wide, 8 * freq * wide),
    )(grads, received, *tables)


def sums_kernel(query_ref, up_ref, conv_ref, out_ref):
    tokens = query_ref.shape[0]
    square = jnp.zeros((tokens, LANES), jnp.float32)
    cross = jnp.zeros((tokens, LANES), jnp.float32)
    for piece in range(conv_ref.shape[0]):
        cols = slice(piece * LANES, (piece + 1) * LANES)
        gated = query_ref[:, cols].astype(jnp.float32) * conv_ref[piece].astype(jnp.float32)
        square += gated * gated
        cross += up_ref[:, cols].astype(jnp.float32) * gated
    out_ref[0:1, :] = jnp.sum(square.T, axis=0, keepdims=True)
    out_ref[1:2, :] = jnp.sum(cross.T, axis=0, keepdims=True)


def token_sums(query, upstream, conv):
    tokens, width = query.shape
    return pl.pallas_call(
        sums_kernel,
        in_specs=whole(3),
        out_specs=pl.BlockSpec(memory_space=pltpu.VMEM),
        out_shape=jax.ShapeDtypeStruct((2, tokens), jnp.float32),
        name="sums",
        **params(5 * tokens * width, 6 * tokens * width),
    )(query, upstream, conv)


def columns_of(channels, own_ref, other_ref, tokens):
    sums = (own_ref[...] + other_ref[...]) / channels
    inverse_row = lax.rsqrt(sums[0:1, :] + 1e-05)
    slope_row = inverse_row * inverse_row * inverse_row * sums[1:2, :]
    inverse = jnp.broadcast_to(inverse_row, (LANES, tokens)).T
    slope = jnp.broadcast_to(slope_row, (LANES, tokens)).T
    return inverse, slope


def grad_kernel(channels, own_ref, other_ref, query_ref, up_ref, conv_ref, grad_ref):
    inverse, slope = columns_of(channels, own_ref, other_ref, query_ref.shape[0])
    for piece in range(conv_ref.shape[0]):
        cols = slice(piece * LANES, (piece + 1) * LANES)
        query = query_ref[:, cols].astype(jnp.float32)
        gated = query * conv_ref[piece].astype(jnp.float32)
        dgated = inverse * up_ref[:, cols].astype(jnp.float32) - slope * gated
        grad_ref[piece] = (dgated * query).astype(jnp.bfloat16)


def norm_kernel(channels, own_ref, other_ref, query_ref, up_ref, conv_ref, mixer_ref, dquery_ref):
    inverse, slope = columns_of(channels, own_ref, other_ref, query_ref.shape[0])
    for piece in range(conv_ref.shape[0]):
        cols = slice(piece * LANES, (piece + 1) * LANES)
        conv = conv_ref[piece].astype(jnp.float32)
        gated = query_ref[:, cols].astype(jnp.float32) * conv
        mixer_ref[:, cols] = (gated * inverse).astype(jnp.bfloat16)
        dgated = inverse * up_ref[:, cols].astype(jnp.float32) - slope * gated
        dquery_ref[:, cols] = (dgated * conv).astype(jnp.bfloat16)


def gate_grad(own, other, query, upstream, conv, channels):
    tokens, width = query.shape

    def kernel(*refs):
        grad_kernel(channels, *refs)

    return pl.pallas_call(
        kernel,
        in_specs=whole(5),
        out_specs=pl.BlockSpec(memory_space=pltpu.VMEM),
        out_shape=jax.ShapeDtypeStruct(conv.shape, jnp.bfloat16),
        name="gate_grad",
        **params(5 * tokens * width, 8 * tokens * width),
    )(own, other, query, upstream, conv)


def gate_norm(own, other, query, upstream, conv, channels):
    tokens, width = query.shape
    step = tokens // 4

    def kernel(own_ref, other_ref, query_ref, up_ref, conv_ref, mixer_ref, dquery_ref, inv_ref, slope_ref):
        i = pl.program_id(0)

        @pl.when(i == 0)
        def _():
            inverse, slope = columns_of(channels, own_ref, other_ref, tokens)
            inv_ref[...] = inverse
            slope_ref[...] = slope

        rows = pl.ds(pl.multiple_of(i * step, step), step)
        inverse, slope = inv_ref[rows, :], slope_ref[rows, :]
        for piece in range(conv_ref.shape[0]):
            cols = slice(piece * LANES, (piece + 1) * LANES)
            conv = conv_ref[piece].astype(jnp.float32)
            gated = query_ref[:, cols].astype(jnp.float32) * conv
            mixer_ref[:, cols] = (gated * inverse).astype(jnp.bfloat16)
            dgated = inverse * up_ref[:, cols].astype(jnp.float32) - slope * gated
            dquery_ref[:, cols] = (dgated * conv).astype(jnp.bfloat16)

    flat = jax.ShapeDtypeStruct((tokens, width), jnp.bfloat16)
    wide = pl.BlockSpec((step, width), lambda i: (i, 0))
    small = pl.BlockSpec((2, tokens), lambda i: (0, 0))
    return pl.pallas_call(
        kernel,
        grid=(4,),
        in_specs=[small, small, wide, wide, pl.BlockSpec((conv.shape[0], step, LANES), lambda i: (0, i, 0))],
        out_specs=[wide, wide],
        out_shape=(flat, flat),
        scratch_shapes=[pltpu.VMEM((tokens, LANES), jnp.float32)] * 2,
        name="norm",
        **params(6 * tokens * width, 10 * tokens * width, 60),
    )(own, other, query, upstream, conv)


def unpack_kernel(
    back_ref, key_ref, value_ref, dkey_hbm, dvalue_hbm, dtaps_hbm, dkey_ref, dvalue_ref, row_sems, tap_sems
):
    tokens = key_ref.shape[0]
    step = tokens // STEPS
    rows = [slice(i * step, (i + 1) * step) for i in range(STEPS)]
    cols = [slice(i * LANES, (i + 1) * LANES) for i in range(back_ref.shape[0])]
    copies = started(
        [
            pltpu.make_async_copy(
                back_ref.at[piece, pl.ds(tokens, tokens)], dtaps_hbm.at[:, col], tap_sems.at[piece]
            )
            for piece, col in enumerate(cols)
        ]
    )
    for i, row in enumerate(rows):
        for piece, col in enumerate(cols):
            dmixed = back_ref[piece, row, :].astype(jnp.float32)
            dkey_ref[row, col] = (dmixed * value_ref[row, col].astype(jnp.float32)).astype(jnp.bfloat16)
            dvalue_ref[row, col] = (dmixed * key_ref[row, col].astype(jnp.float32)).astype(jnp.bfloat16)
        copies += started(
            [
                pltpu.make_async_copy(source.at[row], target.at[row], row_sems.at[which, i])
                for which, (source, target) in enumerate(((dkey_ref, dkey_hbm), (dvalue_ref, dvalue_hbm)))
            ]
        )
    for copy in copies:
        copy.wait()


def unpack(back, key_proj, value_proj):
    tokens, width = key_proj.shape
    flat = jax.ShapeDtypeStruct((tokens, width), jnp.bfloat16)
    return pl.pallas_call(
        unpack_kernel,
        in_specs=whole(3),
        out_specs=[pl.BlockSpec(memory_space=pltpu.HBM)] * 3,
        out_shape=(flat, flat, flat),
        scratch_shapes=[
            pltpu.VMEM((tokens, width), jnp.bfloat16),
            pltpu.VMEM((tokens, width), jnp.bfloat16),
            pltpu.SemaphoreType.DMA((2, STEPS)),
            pltpu.SemaphoreType.DMA((width // LANES,)),
        ],
        name="unpack",
        **params(2 * tokens * width, 14 * tokens * width),
    )(back, key_proj, value_proj)


def exchange(pieces):
    return lax.all_to_all(pieces, "ctx", split_axis=0, concat_axis=0, tiled=True)


def per_device_kernels(query, key_proj, value_proj, filter_taps, grad_out):
    length = query.shape[0] * lax.axis_size("ctx")
    width = query.shape[1] * lax.axis_size("tp")
    block = 2 * query.shape[0]
    scale = 1.0 / (math.sqrt(length) * block)
    tables = odd_tables(block)
    received = exchange(pack(key_proj, value_proj, filter_taps))
    conv = exchange(convolve(received, tables, scale))
    own = token_sums(query, grad_out, conv)
    other = lax.ppermute(own, "tp", [(0, 1), (1, 0)])
    grads = exchange(gate_grad(own, other, query, grad_out, conv, width))
    mixer_out, dquery = gate_norm(own, other, query, grad_out, conv, width)
    back = exchange(correlate(grads, received, tables, scale))
    dkey, dvalue, dtaps = unpack(back, key_proj, value_proj)
    return (mixer_out, dquery, dkey, dvalue, dtaps)


def per_device(query, key_proj, value_proj, filter_taps, grad_out):
    tokens, width = query.shape
    ring = lax.axis_size("ctx")
    pairs = lax.axis_size("tp") == 2
    if pairs and width == ring * LANES and tokens == LANES and ring == 4 * GROUPS:
        return per_device_kernels(query, key_proj, value_proj, filter_taps, grad_out)
    return per_device_plain(query, key_proj, value_proj, filter_taps, grad_out)


def solution(mesh):
    in_specs = (P("ctx", "tp"), P("ctx", "tp"), P("ctx", "tp"), P("ctx", "tp"), P("ctx", "tp"))
    out_specs = (P("ctx", "tp"), P("ctx", "tp"), P("ctx", "tp"), P("ctx", "tp"), P("ctx", "tp"))
    return jax.shard_map(
        per_device, mesh=mesh, in_specs=in_specs, out_specs=out_specs, check_vma=False
    )
```

```python
import math

import jax
import jax.numpy as jnp
import numpy as np
from jax import lax
from jax.experimental import pallas as pl
from jax.experimental.pallas import tpu as pltpu
from jax.sharding import PartitionSpec as P

precise = lax.Precision.HIGHEST


def dft_tables(size_count):
    index = jnp.arange(size_count, dtype=jnp.int32)
    angle = (
        2.0
        * math.pi
        / size_count
        * (index[:, None] * index[None, :] % size_count).astype(jnp.float32)
    )
    return (jnp.cos(angle), jnp.sin(angle))


def twiddles(row_count, col_count):
    total = row_count * col_count
    row_index = jnp.arange(row_count, dtype=jnp.int32)
    col_index = jnp.arange(col_count, dtype=jnp.int32)
    angle = (
        2.0
        * math.pi
        / total
        * (row_index[:, None] * col_index[None, :] % total).astype(jnp.float32)
    )
    return (jnp.cos(angle), jnp.sin(angle))


def left_apply(table, blocks):
    return jnp.einsum("ka,cab->ckb", table, blocks, precision=precise)


def right_apply(blocks, table):
    return jnp.einsum("cka,ab->ckb", blocks, table, precision=precise)


def spectrum(signal):
    channels, length = signal.shape
    total = 2 * length
    row_count = 128
    col_count = total // row_count
    padded = jnp.concatenate(
        [signal.astype(jnp.float32), jnp.zeros((channels, length), jnp.float32)], axis=1
    )
    padded = padded.reshape(channels, row_count, col_count)
    cos_rows, sin_rows = dft_tables(row_count)
    cos_cols, sin_cols = dft_tables(col_count)
    cos_twist, sin_twist = twiddles(row_count, col_count)
    first_real = left_apply(cos_rows, padded)
    first_imag = -left_apply(sin_rows, padded)
    turned_real = first_real * cos_twist + first_imag * sin_twist
    turned_imag = first_imag * cos_twist - first_real * sin_twist
    spec_real = right_apply(turned_real, cos_cols) + right_apply(turned_imag, sin_cols)
    spec_imag = right_apply(turned_imag, cos_cols) - right_apply(turned_real, sin_cols)
    return (spec_real, spec_imag)


def signal_of(spec_real, spec_imag, length):
    channels, row_count, col_count = spec_real.shape
    total = row_count * col_count
    cos_rows, sin_rows = dft_tables(row_count)
    cos_cols, sin_cols = dft_tables(col_count)
    cos_twist, sin_twist = twiddles(row_count, col_count)
    back_real = right_apply(spec_real, cos_cols) - right_apply(spec_imag, sin_cols)
    back_imag = right_apply(spec_imag, cos_cols) + right_apply(spec_real, sin_cols)
    turned_real = back_real * cos_twist - back_imag * sin_twist
    turned_imag = back_imag * cos_twist + back_real * sin_twist
    values = left_apply(cos_rows, turned_real) - left_apply(sin_rows, turned_imag)
    return values.reshape(channels, total)[:, :length] / total


def times_plain(left_real, left_imag, right_real, right_imag):
    return (
        left_real * right_real - left_imag * right_imag,
        left_real * right_imag + left_imag * right_real,
    )


def times_conj(left_real, left_imag, right_real, right_imag):
    return (
        left_real * right_real + left_imag * right_imag,
        left_imag * right_real - left_real * right_imag,
    )


def channel_total(values):
    return lax.psum(values, "tp")


def per_device_plain(query, key_proj, value_proj, filter_taps, grad_out):
    length = query.shape[0] * lax.axis_size("ctx")
    width = query.shape[1] * lax.axis_size("tp")
    filter_scale = 1.0 / math.sqrt(length)
    mixed_rows = (key_proj.astype(jnp.float32) * value_proj.astype(jnp.float32)).astype(
        jnp.bfloat16
    )
    mixed_cols, taps_cols = (
        lax.all_to_all(mixed_rows.T, "ctx", split_axis=0, concat_axis=1, tiled=True),
        lax.all_to_all(filter_taps.T, "ctx", split_axis=0, concat_axis=1, tiled=True),
    )
    taps_real, taps_imag = spectrum(taps_cols)
    mixed_real, mixed_imag = spectrum(mixed_cols)
    conv_real, conv_imag = times_plain(mixed_real, mixed_imag, taps_real, taps_imag)
    conv_cols = (filter_scale * signal_of(conv_real, conv_imag, length)).astype(jnp.bfloat16)
    conv_rows = lax.all_to_all(conv_cols, "ctx", split_axis=1, concat_axis=0, tiled=True).T
    conv_float = conv_rows.astype(jnp.float32)
    query_float = query.astype(jnp.float32)
    gated = query_float * conv_float
    upstream = grad_out.astype(jnp.float32)
    square_sum = channel_total(jnp.sum(gated * gated, axis=1))
    inverse_rms = lax.rsqrt(square_sum / width + 1e-05)
    mixer_out = (gated * inverse_rms[:, None]).astype(jnp.bfloat16)
    dots = channel_total(jnp.sum(upstream * gated, axis=1)) / width
    dgated = inverse_rms[:, None] * upstream - (inverse_rms**3 * dots)[:, None] * gated
    dquery = (dgated * conv_float).astype(jnp.bfloat16)
    gconv = (dgated * query_float).astype(jnp.bfloat16)
    grad_cols = lax.all_to_all(gconv.T, "ctx", split_axis=0, concat_axis=1, tiled=True)
    grad_real, grad_imag = spectrum(grad_cols)
    back_real, back_imag = times_conj(grad_real, grad_imag, taps_real, taps_imag)
    dmixed_cols = (filter_scale * signal_of(back_real, back_imag, length)).astype(jnp.bfloat16)
    tap_real, tap_imag = times_conj(grad_real, grad_imag, mixed_real, mixed_imag)
    dtaps_cols = (filter_scale * signal_of(tap_real, tap_imag, length)).astype(jnp.bfloat16)
    dmixed_back, dtaps_back = (
        lax.all_to_all(dmixed_cols, "ctx", split_axis=1, concat_axis=0, tiled=True),
        lax.all_to_all(dtaps_cols, "ctx", split_axis=1, concat_axis=0, tiled=True),
    )
    dmixed_float = dmixed_back.T.astype(jnp.float32)
    dkey = (dmixed_float * value_proj.astype(jnp.float32)).astype(jnp.bfloat16)
    dvalue = (dmixed_float * key_proj.astype(jnp.float32)).astype(jnp.bfloat16)
    dtaps = dtaps_back.T
    return (mixer_out, dquery, dkey, dvalue, dtaps)


LANES = 128
ROWS = 16
STEPS = 4
GROUPS = 4


def odd_tables(block):
    order = np.concatenate([np.arange(0, block, 2), np.arange(1, block, 2)])
    angle = np.pi * np.outer(2 * order + 1, np.arange(block)) / (2 * block)
    parts = np.stack([np.cos(angle), -np.sin(angle)]).reshape(2, GROUPS, block // GROUPS, block)
    exact = parts.transpose(1, 0, 2, 3).reshape(2 * block, block)
    high = exact.astype(jnp.bfloat16)
    low = (exact - high.astype(np.float64)).astype(jnp.bfloat16)
    return jnp.asarray(np.concatenate([high, low], axis=1)), jnp.asarray(high.T.copy())


def params(flops, moved, limit=16):
    return dict(
        compiler_params=pltpu.CompilerParams(vmem_limit_bytes=limit * 2**20),
        cost_estimate=pl.CostEstimate(flops=flops, bytes_accessed=moved, transcendentals=0),
    )


def whole(count):
    return [pl.BlockSpec(memory_space=pltpu.VMEM)] * count


def started(copies):
    for copy in copies:
        copy.start()
    return copies


def pack_kernel(
    key_hbm, value_hbm, taps_hbm, out_hbm, key_ref, value_ref, taps_ref, stage_ref, in_sems, out_sems
):
    pieces = stage_ref.shape[0]
    share = pieces // STEPS
    loads = []
    for i in range(STEPS):
        wide = slice(i * share * LANES, (i + 1) * share * LANES)
        group = [
            pltpu.make_async_copy(key_hbm.at[:, wide], key_ref.at[:, wide], in_sems.at[0, i]),
            pltpu.make_async_copy(value_hbm.at[:, wide], value_ref.at[:, wide], in_sems.at[1, i]),
        ]
        group.append(pltpu.make_async_copy(taps_hbm.at[:, wide], taps_ref.at[:, wide], in_sems.at[2, i]))
        loads.append(started(group))
    stores = []
    for i, group in enumerate(loads):
        for copy in group:
            copy.wait()
        for piece in range(i * share, (i + 1) * share):
            col = slice(piece * LANES, (piece + 1) * LANES)
            product = key_ref[:, col].astype(jnp.float32) * value_ref[:, col].astype(jnp.float32)
            stage_ref[piece, 0] = product.astype(jnp.bfloat16)
            stage_ref[piece, 1] = taps_ref[:, col]
        part = pl.ds(i * share, share)
        stores += started([pltpu.make_async_copy(stage_ref.at[part], out_hbm.at[part], out_sems.at[i])])
    for copy in stores:
        copy.wait()


def pack(key_proj, value_proj, taps):
    tokens, width = key_proj.shape
    pieces = width // LANES
    packed = pl.pallas_call(
        pack_kernel,
        in_specs=[pl.BlockSpec(memory_space=pltpu.HBM)] * 3,
        out_specs=pl.BlockSpec(memory_space=pltpu.HBM),
        out_shape=jax.ShapeDtypeStruct((pieces, 2, tokens, LANES), jnp.bfloat16),
        scratch_shapes=[
            pltpu.VMEM((tokens, width), jnp.bfloat16),
            pltpu.VMEM((tokens, width), jnp.bfloat16),
            pltpu.VMEM((tokens, width), jnp.bfloat16),
            pltpu.VMEM((pieces, 2, tokens, LANES), jnp.bfloat16),
            pltpu.SemaphoreType.DMA((3, STEPS)),
            pltpu.SemaphoreType.DMA((STEPS,)),
        ],
        name="pack",
        **params(tokens * width, 10 * tokens * width, 63),
    )(key_proj, value_proj, taps)
    return packed.reshape(pieces, 2 * tokens, LANES)


def transform(table_ref, spec_ref, group, in_ref, offset, tokens, tile):
    block = table_ref.shape[1] // 2
    per = block // tokens
    blocks = []
    for b in range(2):
        parts = [
            in_ref[(2 * tile + b) * per + p, offset : offset + tokens, :] for p in range(per)
        ]
        blocks.append(jnp.concatenate(parts + parts, axis=0))
    columns = jnp.concatenate(blocks, axis=1)
    size = spec_ref.shape[0]
    rows = table_ref[group * size : (group + 1) * size, :]
    lanes = pl.ds(tile * 2 * LANES, 2 * LANES)
    spec_ref[:, lanes] = jnp.dot(rows, columns, preferred_element_type=jnp.float32)


def restore(back_ref, acc_ref, out_ref, offset, tokens, scale, tile):
    per = back_ref.shape[0] // tokens
    lanes = slice(tile * 2 * LANES, (tile + 1) * 2 * LANES)
    signal = jnp.dot(back_ref[...], acc_ref[:, lanes], preferred_element_type=jnp.float32)
    rounded = (signal * scale).astype(jnp.bfloat16)
    for b in range(2):
        for p in range(per):
            out_ref[(2 * tile + b) * per + p, offset : offset + tokens, :] = rounded[
                p * tokens : (p + 1) * tokens, b * LANES : (b + 1) * LANES
            ]


def tile_of(ref, row, b):
    half = ref.shape[0] // 2
    cols = slice(b * LANES, (b + 1) * LANES)
    return (ref[pl.ds(row, ROWS), cols], ref[pl.ds(row + half, ROWS), cols])


def put_tile(ref, group, row, b, real, imag):
    size = ref.shape[0] // GROUPS
    cols = slice(b * LANES, (b + 1) * LANES)
    ref[pl.ds(group * size + row, ROWS), cols] = real.astype(ref.dtype)
    ref[pl.ds(group * size + size // 2 + row, ROWS), cols] = imag.astype(ref.dtype)


def plus(total, term):
    return term if total is None else total + term


def forward_products(mix_ref, tap_ref, acc_ref, group, row):
    count = mix_ref.shape[1] // LANES
    taps = [tile_of(tap_ref, row, b) for b in range(count)]
    taps = [(r, i, r + i) for r, i in taps]
    mixes = [tile_of(mix_ref, row, b) for b in range(count)]
    mixes = [(r, i, r + i) for r, i in mixes]
    before = None
    for d in range(count):
        first = second = third = None
        for j in range(d + 1):
            mr, mi, ms = mixes[j]
            tr, ti, ts = taps[d - j]
            first = plus(first, mr * tr)
            second = plus(second, mi * ti)
            third = plus(third, ms * ts)
        real = first - second
        imag = third - first - second
        if before is None:
            put_tile(acc_ref, group, row, d, real, imag)
        elif group < GROUPS // 2:
            put_tile(acc_ref, group, row, d, real - before[1], imag + before[0])
        else:
            put_tile(acc_ref, group, row, d, real + before[1], imag - before[0])
        before = (real, imag)


def backward_products(grad_ref, other_ref, acc_ref, group, row):
    count = grad_ref.shape[1] // LANES
    others = [tile_of(other_ref, row, b) for b in range(count)]
    others = [(r, i, r - i) for r, i in others]
    grads = [tile_of(grad_ref, row, b) for b in range(count)]
    grads = [(r, i, r + i) for r, i in grads]
    after = None
    for d in reversed(range(count)):
        first = second = third = None
        for k in range(count - d):
            gr, gi, gs = grads[d + k]
            ar, ai, ad = others[k]
            first = plus(first, gr * ar)
            second = plus(second, gi * ai)
            third = plus(third, gs * ad)
        real = first + second
        imag = third - first + second
        if after is None:
            put_tile(acc_ref, group, row, d, real, imag)
        elif group < GROUPS // 2:
            put_tile(acc_ref, group, row, d, real + after[1], imag - after[0])
        else:
            put_tile(acc_ref, group, row, d, real - after[1], imag + after[0])
        after = (real, imag)


def each_step(count, body):
    for i in range(count):
        body(i)


def forward_kernel(scale, in_ref, table_ref, back_ref, out_ref, acc_ref, *spectra):
    mixes, taps = spectra[:GROUPS], spectra[GROUPS:]
    tokens = out_ref.shape[1]
    tiles = acc_ref.shape[1] // (2 * LANES)

    def transforms(group, tile):
        transform(table_ref, mixes[group], group, in_ref, 0, tokens, tile)
        transform(table_ref, taps[group], group, in_ref, tokens, tokens, tile)

    for tile in range(tiles):
        transforms(0, tile)
    for group in range(GROUPS):

        def step(i, group=group):
            row = i * ROWS
            if group + 1 < GROUPS:
                transforms(group + 1, i)
            forward_products(mixes[group], taps[group], acc_ref, group, row)

        each_step(tiles, step)
    for tile in range(tiles):
        restore(back_ref, acc_ref, out_ref, 0, tokens, scale, tile)


def backward_kernel(
    scale, grad_in_ref, in_ref, table_ref, back_ref, out_hbm, out_ref, sems, mixed_ref, dtaps_ref, *spectra
):
    grads, taps, mixes = spectra[:GROUPS], spectra[GROUPS : 2 * GROUPS], spectra[2 * GROUPS :]
    tokens = grad_in_ref.shape[1]
    tiles = mixed_ref.shape[1] // (2 * LANES)

    copies = []

    def send(offset, which, tile):
        share = out_ref.shape[0] // tiles
        part = (pl.ds(tile * share, share), pl.ds(offset, tokens))
        copies.extend(
            started([pltpu.make_async_copy(out_ref.at[part], out_hbm.at[part], sems.at[which, tile])])
        )

    def transforms(group, tile):
        transform(table_ref, grads[group], group, grad_in_ref, 0, tokens, tile)
        transform(table_ref, taps[group], group, in_ref, tokens, tokens, tile)

    for tile in range(tiles):
        transforms(0, tile)
    for group in range(GROUPS):

        def step(i, group=group):
            row = i * ROWS
            if group + 1 < GROUPS:
                transforms(group + 1, i)
            transform(table_ref, mixes[group], group, in_ref, 0, tokens, i)
            backward_products(grads[group], taps[group], mixed_ref, group, row)

        each_step(tiles, step)
    for group in range(GROUPS):

        def step(i, group=group):
            row = i * ROWS
            if i == 0:
                restore(back_ref, mixed_ref, out_ref, 0, tokens, scale, group)
                send(0, 0, group)
            backward_products(grads[group], mixes[group], dtaps_ref, group, row)

        each_step(tiles, step)
    for tile in range(tiles):
        restore(back_ref, dtaps_ref, out_ref, tokens, tokens, scale, tile)
        send(tokens, 1, tile)
    for copy in copies:
        copy.wait()


def convolve(received, tables, scale):
    pieces, rows, _ = received.shape
    tokens = rows // 2
    block, freq = tables[1].shape
    wide = pieces * tokens // block * LANES

    def kernel(*refs):
        forward_kernel(scale, *refs)

    return pl.pallas_call(
        kernel,
        in_specs=whole(3),
        out_specs=pl.BlockSpec(memory_space=pltpu.VMEM),
        out_shape=jax.ShapeDtypeStruct((pieces, tokens, LANES), jnp.bfloat16),
        scratch_shapes=[pltpu.VMEM((freq, wide), jnp.bfloat16)]
        + [pltpu.VMEM((freq // GROUPS, wide), jnp.float32)] * (2 * GROUPS),
        name="forward",
        **params(10 * freq * block * wide, 8 * freq * wide),
    )(received, *tables)


def correlate(grads, received, tables, scale):
    pieces, tokens, _ = grads.shape
    block, freq = tables[1].shape
    wide = pieces * tokens // block * LANES

    def kernel(*refs):
        backward_kernel(scale, *refs)

    return pl.pallas_call(
        kernel,
        in_specs=whole(4),
        out_specs=pl.BlockSpec(memory_space=pltpu.HBM),
        out_shape=jax.ShapeDtypeStruct((pieces, 2 * tokens, LANES), jnp.bfloat16),
        scratch_shapes=[
            pltpu.VMEM((pieces, 2 * tokens, LANES), jnp.bfloat16),
            pltpu.SemaphoreType.DMA((2, GROUPS)),
        ]
        + [pltpu.VMEM((freq, wide), jnp.bfloat16)] * 2
        + [pltpu.VMEM((freq // GROUPS, wide), jnp.float32)] * (3 * GROUPS),
        name="backward",
        **params(16 * freq * block * wide, 8 * freq * wide),
    )(grads, received, *tables)


def sums_kernel(query_ref, up_ref, conv_ref, out_ref):
    tokens = query_ref.shape[0]
    square = jnp.zeros((tokens, LANES), jnp.float32)
    cross = jnp.zeros((tokens, LANES), jnp.float32)
    for piece in range(conv_ref.shape[0]):
        cols = slice(piece * LANES, (piece + 1) * LANES)
        gated = query_ref[:, cols].astype(jnp.float32) * conv_ref[piece].astype(jnp.float32)
        square += gated * gated
        cross += up_ref[:, cols].astype(jnp.float32) * gated
    out_ref[0:1, :] = jnp.sum(square.T, axis=0, keepdims=True)
    out_ref[1:2, :] = jnp.sum(cross.T, axis=0, keepdims=True)


def token_sums(query, upstream, conv):
    tokens, width = query.shape
    return pl.pallas_call(
        sums_kernel,
        in_specs=whole(3),
        out_specs=pl.BlockSpec(memory_space=pltpu.VMEM),
        out_shape=jax.ShapeDtypeStruct((2, tokens), jnp.float32),
        name="sums",
        **params(5 * tokens * width, 6 * tokens * width),
    )(query, upstream, conv)


def columns_of(channels, own_ref, other_ref, tokens):
    sums = (own_ref[...] + other_ref[...]) / channels
    inverse_row = lax.rsqrt(sums[0:1, :] + 1e-05)
    slope_row = inverse_row * inverse_row * inverse_row * sums[1:2, :]
    inverse = jnp.broadcast_to(inverse_row, (LANES, tokens)).T
    slope = jnp.broadcast_to(slope_row, (LANES, tokens)).T
    return inverse, slope


def grad_kernel(channels, own_ref, other_ref, query_ref, up_ref, conv_ref, grad_ref):
    inverse, slope = columns_of(channels, own_ref, other_ref, query_ref.shape[0])
    for piece in range(conv_ref.shape[0]):
        cols = slice(piece * LANES, (piece + 1) * LANES)
        query = query_ref[:, cols].astype(jnp.float32)
        gated = query * conv_ref[piece].astype(jnp.float32)
        dgated = inverse * up_ref[:, cols].astype(jnp.float32) - slope * gated
        grad_ref[piece] = (dgated * query).astype(jnp.bfloat16)


def norm_kernel(channels, own_ref, other_ref, query_ref, up_ref, conv_ref, mixer_ref, dquery_ref):
    inverse, slope = columns_of(channels, own_ref, other_ref, query_ref.shape[0])
    for piece in range(conv_ref.shape[0]):
        cols = slice(piece * LANES, (piece + 1) * LANES)
        conv = conv_ref[piece].astype(jnp.float32)
        gated = query_ref[:, cols].astype(jnp.float32) * conv
        mixer_ref[:, cols] = (gated * inverse).astype(jnp.bfloat16)
        dgated = inverse * up_ref[:, cols].astype(jnp.float32) - slope * gated
        dquery_ref[:, cols] = (dgated * conv).astype(jnp.bfloat16)


def gate_grad(own, other, query, upstream, conv, channels):
    tokens, width = query.shape

    def kernel(*refs):
        grad_kernel(channels, *refs)

    return pl.pallas_call(
        kernel,
        in_specs=whole(5),
        out_specs=pl.BlockSpec(memory_space=pltpu.VMEM),
        out_shape=jax.ShapeDtypeStruct(conv.shape, jnp.bfloat16),
        name="gate_grad",
        **params(5 * tokens * width, 8 * tokens * width),
    )(own, other, query, upstream, conv)


def gate_norm(own, other, query, upstream, conv, channels):
    tokens, width = query.shape
    step = tokens // 4

    def kernel(own_ref, other_ref, query_ref, up_ref, conv_ref, mixer_ref, dquery_ref, inv_ref, slope_ref):
        i = pl.program_id(0)

        @pl.when(i == 0)
        def _():
            inverse, slope = columns_of(channels, own_ref, other_ref, tokens)
            inv_ref[...] = inverse
            slope_ref[...] = slope

        rows = pl.ds(pl.multiple_of(i * step, step), step)
        inverse, slope = inv_ref[rows, :], slope_ref[rows, :]
        for piece in range(conv_ref.shape[0]):
            cols = slice(piece * LANES, (piece + 1) * LANES)
            conv = conv_ref[piece].astype(jnp.float32)
            gated = query_ref[:, cols].astype(jnp.float32) * conv
            mixer_ref[:, cols] = (gated * inverse).astype(jnp.bfloat16)
            dgated = inverse * up_ref[:, cols].astype(jnp.float32) - slope * gated
            dquery_ref[:, cols] = (dgated * conv).astype(jnp.bfloat16)

    flat = jax.ShapeDtypeStruct((tokens, width), jnp.bfloat16)
    wide = pl.BlockSpec((step, width), lambda i: (i, 0))
    small = pl.BlockSpec((2, tokens), lambda i: (0, 0))
    return pl.pallas_call(
        kernel,
        grid=(4,),
        in_specs=[small, small, wide, wide, pl.BlockSpec((conv.shape[0], step, LANES), lambda i: (0, i, 0))],
        out_specs=[wide, wide],
        out_shape=(flat, flat),
        scratch_shapes=[pltpu.VMEM((tokens, LANES), jnp.float32)] * 2,
        name="norm",
        **params(6 * tokens * width, 10 * tokens * width, 60),
    )(own, other, query, upstream, conv)


def unpack_kernel(
    back_ref, key_ref, value_ref, dkey_hbm, dvalue_hbm, dtaps_hbm, dkey_ref, dvalue_ref, row_sems, tap_sems
):
    tokens = key_ref.shape[0]
    step = tokens // STEPS
    rows = [slice(i * step, (i + 1) * step) for i in range(STEPS)]
    cols = [slice(i * LANES, (i + 1) * LANES) for i in range(back_ref.shape[0])]
    copies = started(
        [
            pltpu.make_async_copy(
                back_ref.at[piece, pl.ds(tokens, tokens)], dtaps_hbm.at[:, col], tap_sems.at[piece]
            )
            for piece, col in enumerate(cols)
        ]
    )
    for i, row in enumerate(rows):
        for piece, col in enumerate(cols):
            dmixed = back_ref[piece, row, :].astype(jnp.float32)
            dkey_ref[row, col] = (dmixed * value_ref[row, col].astype(jnp.float32)).astype(jnp.bfloat16)
            dvalue_ref[row, col] = (dmixed * key_ref[row, col].astype(jnp.float32)).astype(jnp.bfloat16)
        copies += started(
            [
                pltpu.make_async_copy(source.at[row], target.at[row], row_sems.at[which, i])
                for which, (source, target) in enumerate(((dkey_ref, dkey_hbm), (dvalue_ref, dvalue_hbm)))
            ]
        )
    for copy in copies:
        copy.wait()


def unpack(back, key_proj, value_proj):
    tokens, width = key_proj.shape
    flat = jax.ShapeDtypeStruct((tokens, width), jnp.bfloat16)
    return pl.pallas_call(
        unpack_kernel,
        in_specs=whole(3),
        out_specs=[pl.BlockSpec(memory_space=pltpu.HBM)] * 3,
        out_shape=(flat, flat, flat),
        scratch_shapes=[
            pltpu.VMEM((tokens, width), jnp.bfloat16),
            pltpu.VMEM((tokens, width), jnp.bfloat16),
            pltpu.SemaphoreType.DMA((2, STEPS)),
            pltpu.SemaphoreType.DMA((width // LANES,)),
        ],
        name="unpack",
        **params(2 * tokens * width, 14 * tokens * width),
    )(back, key_proj, value_proj)


def exchange(pieces):
    return lax.all_to_all(pieces, "ctx", split_axis=0, concat_axis=0, tiled=True)


def per_device_kernels(query, key_proj, value_proj, filter_taps, grad_out):
    length = query.shape[0] * lax.axis_size("ctx")
    width = query.shape[1] * lax.axis_size("tp")
    block = 2 * query.shape[0]
    scale = 1.0 / (math.sqrt(length) * block)
    tables = odd_tables(block)
    received = exchange(pack(key_proj, value_proj, filter_taps))
    conv = exchange(convolve(received, tables, scale))
    own = token_sums(query, grad_out, conv)
    other = lax.ppermute(own, "tp", [(0, 1), (1, 0)])
    grads = exchange(gate_grad(own, other, query, grad_out, conv, width))
    mixer_out, dquery = gate_norm(own, other, query, grad_out, conv, width)
    back = exchange(correlate(grads, received, tables, scale))
    dkey, dvalue, dtaps = unpack(back, key_proj, value_proj)
    return (mixer_out, dquery, dkey, dvalue, dtaps)


def per_device(query, key_proj, value_proj, filter_taps, grad_out):
    tokens, width = query.shape
    ring = lax.axis_size("ctx")
    pairs = lax.axis_size("tp") == 2
    if pairs and width == ring * LANES and tokens == LANES and ring == 4 * GROUPS:
        return per_device_kernels(query, key_proj, value_proj, filter_taps, grad_out)
    return per_device_plain(query, key_proj, value_proj, filter_taps, grad_out)


def solution(mesh):
    in_specs = (P("ctx", "tp"), P("ctx", "tp"), P("ctx", "tp"), P("ctx", "tp"), P("ctx", "tp"))
    out_specs = (P("ctx", "tp"), P("ctx", "tp"), P("ctx", "tp"), P("ctx", "tp"), P("ctx", "tp"))
    return jax.shard_map(
        per_device, mesh=mesh, in_specs=in_specs, out_specs=out_specs, check_vma=False
    )
```

```python
import math

import jax
import jax.numpy as jnp
import numpy as np
from jax import lax
from jax.experimental import pallas as pl
from jax.experimental.pallas import tpu as pltpu
from jax.sharding import PartitionSpec as P

precise = lax.Precision.HIGHEST


def dft_tables(size_count):
    index = jnp.arange(size_count, dtype=jnp.int32)
    angle = (
        2.0
        * math.pi
        / size_count
        * (index[:, None] * index[None, :] % size_count).astype(jnp.float32)
    )
    return (jnp.cos(angle), jnp.sin(angle))


def twiddles(row_count, col_count):
    total = row_count * col_count
    row_index = jnp.arange(row_count, dtype=jnp.int32)
    col_index = jnp.arange(col_count, dtype=jnp.int32)
    angle = (
        2.0
        * math.pi
        / total
        * (row_index[:, None] * col_index[None, :] % total).astype(jnp.float32)
    )
    return (jnp.cos(angle), jnp.sin(angle))


def left_apply(table, blocks):
    return jnp.einsum("ka,cab->ckb", table, blocks, precision=precise)


def right_apply(blocks, table):
    return jnp.einsum("cka,ab->ckb", blocks, table, precision=precise)


def spectrum(signal):
    channels, length = signal.shape
    total = 2 * length
    row_count = 128
    col_count = total // row_count
    padded = jnp.concatenate(
        [signal.astype(jnp.float32), jnp.zeros((channels, length), jnp.float32)], axis=1
    )
    padded = padded.reshape(channels, row_count, col_count)
    cos_rows, sin_rows = dft_tables(row_count)
    cos_cols, sin_cols = dft_tables(col_count)
    cos_twist, sin_twist = twiddles(row_count, col_count)
    first_real = left_apply(cos_rows, padded)
    first_imag = -left_apply(sin_rows, padded)
    turned_real = first_real * cos_twist + first_imag * sin_twist
    turned_imag = first_imag * cos_twist - first_real * sin_twist
    spec_real = right_apply(turned_real, cos_cols) + right_apply(turned_imag, sin_cols)
    spec_imag = right_apply(turned_imag, cos_cols) - right_apply(turned_real, sin_cols)
    return (spec_real, spec_imag)


def signal_of(spec_real, spec_imag, length):
    channels, row_count, col_count = spec_real.shape
    total = row_count * col_count
    cos_rows, sin_rows = dft_tables(row_count)
    cos_cols, sin_cols = dft_tables(col_count)
    cos_twist, sin_twist = twiddles(row_count, col_count)
    back_real = right_apply(spec_real, cos_cols) - right_apply(spec_imag, sin_cols)
    back_imag = right_apply(spec_imag, cos_cols) + right_apply(spec_real, sin_cols)
    turned_real = back_real * cos_twist - back_imag * sin_twist
    turned_imag = back_imag * cos_twist + back_real * sin_twist
    values = left_apply(cos_rows, turned_real) - left_apply(sin_rows, turned_imag)
    return values.reshape(channels, total)[:, :length] / total


def times_plain(left_real, left_imag, right_real, right_imag):
    return (
        left_real * right_real - left_imag * right_imag,
        left_real * right_imag + left_imag * right_real,
    )


def times_conj(left_real, left_imag, right_real, right_imag):
    return (
        left_real * right_real + left_imag * right_imag,
        left_imag * right_real - left_real * right_imag,
    )


def channel_total(values):
    return lax.psum(values, "tp")


def per_device_plain(query, key_proj, value_proj, filter_taps, grad_out):
    length = query.shape[0] * lax.axis_size("ctx")
    width = query.shape[1] * lax.axis_size("tp")
    filter_scale = 1.0 / math.sqrt(length)
    mixed_rows = (key_proj.astype(jnp.float32) * value_proj.astype(jnp.float32)).astype(
        jnp.bfloat16
    )
    mixed_cols, taps_cols = (
        lax.all_to_all(mixed_rows.T, "ctx", split_axis=0, concat_axis=1, tiled=True),
        lax.all_to_all(filter_taps.T, "ctx", split_axis=0, concat_axis=1, tiled=True),
    )
    taps_real, taps_imag = spectrum(taps_cols)
    mixed_real, mixed_imag = spectrum(mixed_cols)
    conv_real, conv_imag = times_plain(mixed_real, mixed_imag, taps_real, taps_imag)
    conv_cols = (filter_scale * signal_of(conv_real, conv_imag, length)).astype(jnp.bfloat16)
    conv_rows = lax.all_to_all(conv_cols, "ctx", split_axis=1, concat_axis=0, tiled=True).T
    conv_float = conv_rows.astype(jnp.float32)
    query_float = query.astype(jnp.float32)
    gated = query_float * conv_float
    upstream = grad_out.astype(jnp.float32)
    square_sum = channel_total(jnp.sum(gated * gated, axis=1))
    inverse_rms = lax.rsqrt(square_sum / width + 1e-05)
    mixer_out = (gated * inverse_rms[:, None]).astype(jnp.bfloat16)
    dots = channel_total(jnp.sum(upstream * gated, axis=1)) / width
    dgated = inverse_rms[:, None] * upstream - (inverse_rms**3 * dots)[:, None] * gated
    dquery = (dgated * conv_float).astype(jnp.bfloat16)
    gconv = (dgated * query_float).astype(jnp.bfloat16)
    grad_cols = lax.all_to_all(gconv.T, "ctx", split_axis=0, concat_axis=1, tiled=True)
    grad_real, grad_imag = spectrum(grad_cols)
    back_real, back_imag = times_conj(grad_real, grad_imag, taps_real, taps_imag)
    dmixed_cols = (filter_scale * signal_of(back_real, back_imag, length)).astype(jnp.bfloat16)
    tap_real, tap_imag = times_conj(grad_real, grad_imag, mixed_real, mixed_imag)
    dtaps_cols = (filter_scale * signal_of(tap_real, tap_imag, length)).astype(jnp.bfloat16)
    dmixed_back, dtaps_back = (
        lax.all_to_all(dmixed_cols, "ctx", split_axis=1, concat_axis=0, tiled=True),
        lax.all_to_all(dtaps_cols, "ctx", split_axis=1, concat_axis=0, tiled=True),
    )
    dmixed_float = dmixed_back.T.astype(jnp.float32)
    dkey = (dmixed_float * value_proj.astype(jnp.float32)).astype(jnp.bfloat16)
    dvalue = (dmixed_float * key_proj.astype(jnp.float32)).astype(jnp.bfloat16)
    dtaps = dtaps_back.T
    return (mixer_out, dquery, dkey, dvalue, dtaps)


LANES = 128
ROWS = 16
STEPS = 4
GROUPS = 4


def odd_tables(block):
    order = np.concatenate([np.arange(0, block, 2), np.arange(1, block, 2)])
    angle = np.pi * np.outer(2 * order + 1, np.arange(block)) / (2 * block)
    parts = np.stack([np.cos(angle), -np.sin(angle)]).reshape(2, GROUPS, block // GROUPS, block)
    forward = parts.transpose(1, 0, 2, 3).reshape(2 * block, block).astype(jnp.bfloat16)
    return jnp.asarray(forward), jnp.asarray(forward.T.copy())


def params(flops, moved, limit=16):
    return dict(
        compiler_params=pltpu.CompilerParams(vmem_limit_bytes=limit * 2**20),
        cost_estimate=pl.CostEstimate(flops=flops, bytes_accessed=moved, transcendentals=0),
    )


def whole(count):
    return [pl.BlockSpec(memory_space=pltpu.VMEM)] * count


def started(copies):
    for copy in copies:
        copy.start()
    return copies


def pack_kernel(
    key_hbm, value_hbm, taps_hbm, out_hbm, key_ref, value_ref, taps_ref, stage_ref, in_sems, out_sems
):
    pieces = stage_ref.shape[0]
    share = pieces // STEPS
    loads = []
    for i in range(STEPS):
        wide = slice(i * share * LANES, (i + 1) * share * LANES)
        group = [
            pltpu.make_async_copy(key_hbm.at[:, wide], key_ref.at[:, wide], in_sems.at[0, i]),
            pltpu.make_async_copy(value_hbm.at[:, wide], value_ref.at[:, wide], in_sems.at[1, i]),
        ]
        group.append(pltpu.make_async_copy(taps_hbm.at[:, wide], taps_ref.at[:, wide], in_sems.at[2, i]))
        loads.append(started(group))
    stores = []
    for i, group in enumerate(loads):
        for copy in group:
            copy.wait()
        for piece in range(i * share, (i + 1) * share):
            col = slice(piece * LANES, (piece + 1) * LANES)
            product = key_ref[:, col].astype(jnp.float32) * value_ref[:, col].astype(jnp.float32)
            stage_ref[piece, 0] = product.astype(jnp.bfloat16)
            stage_ref[piece, 1] = taps_ref[:, col]
        part = pl.ds(i * share, share)
        stores += started([pltpu.make_async_copy(stage_ref.at[part], out_hbm.at[part], out_sems.at[i])])
    for copy in stores:
        copy.wait()


def pack(key_proj, value_proj, taps):
    tokens, width = key_proj.shape
    pieces = width // LANES
    packed = pl.pallas_call(
        pack_kernel,
        in_specs=[pl.BlockSpec(memory_space=pltpu.HBM)] * 3,
        out_specs=pl.BlockSpec(memory_space=pltpu.HBM),
        out_shape=jax.ShapeDtypeStruct((pieces, 2, tokens, LANES), jnp.bfloat16),
        scratch_shapes=[
            pltpu.VMEM((tokens, width), jnp.bfloat16),
            pltpu.VMEM((tokens, width), jnp.bfloat16),
            pltpu.VMEM((tokens, width), jnp.bfloat16),
            pltpu.VMEM((pieces, 2, tokens, LANES), jnp.bfloat16),
            pltpu.SemaphoreType.DMA((3, STEPS)),
            pltpu.SemaphoreType.DMA((STEPS,)),
        ],
        name="pack",
        **params(tokens * width, 10 * tokens * width, 63),
    )(key_proj, value_proj, taps)
    return packed.reshape(pieces, 2 * tokens, LANES)


def transform(table_ref, spec_ref, group, in_ref, offset, tokens, tile):
    block = table_ref.shape[1]
    per = block // tokens
    blocks = []
    for b in range(2):
        parts = [
            in_ref[(2 * tile + b) * per + p, offset : offset + tokens, :] for p in range(per)
        ]
        blocks.append(jnp.concatenate(parts, axis=0))
    columns = jnp.concatenate(blocks, axis=1)
    size = spec_ref.shape[0]
    rows = table_ref[group * size : (group + 1) * size, :]
    lanes = pl.ds(tile * 2 * LANES, 2 * LANES)
    spec_ref[:, lanes] = jnp.dot(rows, columns, preferred_element_type=jnp.float32)


def restore(back_ref, acc_ref, out_ref, offset, tokens, scale, tile):
    per = back_ref.shape[0] // tokens
    lanes = slice(tile * 2 * LANES, (tile + 1) * 2 * LANES)
    signal = jnp.dot(back_ref[...], acc_ref[:, lanes], preferred_element_type=jnp.float32)
    rounded = (signal * scale).astype(jnp.bfloat16)
    for b in range(2):
        for p in range(per):
            out_ref[(2 * tile + b) * per + p, offset : offset + tokens, :] = rounded[
                p * tokens : (p + 1) * tokens, b * LANES : (b + 1) * LANES
            ]


def tile_of(ref, row, b):
    half = ref.shape[0] // 2
    cols = slice(b * LANES, (b + 1) * LANES)
    return (ref[pl.ds(row, ROWS), cols], ref[pl.ds(row + half, ROWS), cols])


def put_tile(ref, group, row, b, real, imag):
    size = ref.shape[0] // GROUPS
    cols = slice(b * LANES, (b + 1) * LANES)
    ref[pl.ds(group * size + row, ROWS), cols] = real.astype(ref.dtype)
    ref[pl.ds(group * size + size // 2 + row, ROWS), cols] = imag.astype(ref.dtype)


def plus(total, term):
    return term if total is None else total + term


def forward_products(mix_ref, tap_ref, acc_ref, group, row):
    count = mix_ref.shape[1] // LANES
    taps = [tile_of(tap_ref, row, b) for b in range(count)]
    taps = [(r, i, r + i) for r, i in taps]
    mixes = [tile_of(mix_ref, row, b) for b in range(count)]
    mixes = [(r, i, r + i) for r, i in mixes]
    before = None
    for d in range(count):
        first = second = third = None
        for j in range(d + 1):
            mr, mi, ms = mixes[j]
            tr, ti, ts = taps[d - j]
            first = plus(first, mr * tr)
            second = plus(second, mi * ti)
            third = plus(third, ms * ts)
        real = first - second
        imag = third - first - second
        if before is None:
            put_tile(acc_ref, group, row, d, real, imag)
        elif group < GROUPS // 2:
            put_tile(acc_ref, group, row, d, real - before[1], imag + before[0])
        else:
            put_tile(acc_ref, group, row, d, real + before[1], imag - before[0])
        before = (real, imag)


def backward_products(grad_ref, other_ref, acc_ref, group, row, first_block, last_block):
    count = grad_ref.shape[1] // LANES
    others = [tile_of(other_ref, row, b) for b in range(count)]
    others = [(r, i, r - i) for r, i in others]
    grads = [tile_of(grad_ref, row, b) for b in range(count)]
    grads = [(r, i, r + i) for r, i in grads]
    after = None
    for d in reversed(range(first_block, min(last_block + 1, count))):
        first = second = third = None
        for k in range(count - d):
            gr, gi, gs = grads[d + k]
            ar, ai, ad = others[k]
            first = plus(first, gr * ar)
            second = plus(second, gi * ai)
            third = plus(third, gs * ad)
        real = first + second
        imag = third - first + second
        if d == last_block:
            pass
        elif after is None:
            put_tile(acc_ref, group, row, d, real, imag)
        elif group < GROUPS // 2:
            put_tile(acc_ref, group, row, d, real + after[1], imag - after[0])
        else:
            put_tile(acc_ref, group, row, d, real - after[1], imag + after[0])
        after = (real, imag)


def each_step(count, body):
    for i in range(count):
        body(i)


def forward_kernel(scale, in_ref, table_ref, back_ref, out_ref, acc_ref, *spectra):
    mixes, taps = spectra[:GROUPS], spectra[GROUPS:]
    tokens = out_ref.shape[1]
    tiles = acc_ref.shape[1] // (2 * LANES)

    def transforms(group, tile):
        transform(table_ref, mixes[group], group, in_ref, 0, tokens, tile)
        transform(table_ref, taps[group], group, in_ref, tokens, tokens, tile)

    for tile in range(tiles):
        transforms(0, tile)
    for group in range(GROUPS):

        def step(i, group=group):
            row = i * ROWS
            if group + 1 < GROUPS:
                transforms(group + 1, i)
            forward_products(mixes[group], taps[group], acc_ref, group, row)

        each_step(tiles, step)
    for tile in range(tiles):
        restore(back_ref, acc_ref, out_ref, 0, tokens, scale, tile)


def backward_kernel(
    scale, grad_in_ref, in_ref, table_ref, back_ref, out_hbm, out_ref, sems, mixed_ref, dtaps_ref, *spectra
):
    grads, taps, mixes = spectra[:GROUPS], spectra[GROUPS : 2 * GROUPS], spectra[2 * GROUPS :]
    tokens = grad_in_ref.shape[1]
    tiles = mixed_ref.shape[1] // (2 * LANES)

    copies = []

    def send(offset, which, tile):
        share = out_ref.shape[0] // tiles
        part = (pl.ds(tile * share, share), pl.ds(offset, tokens))
        copies.extend(
            started([pltpu.make_async_copy(out_ref.at[part], out_hbm.at[part], sems.at[which, tile])])
        )

    def transforms(group, tile):
        transform(table_ref, grads[group], group, grad_in_ref, 0, tokens, tile)
        transform(table_ref, taps[group], group, in_ref, tokens, tokens, tile)

    for tile in range(tiles):
        transforms(0, tile)
    for group in range(GROUPS):

        def step(i, group=group):
            row = i * ROWS
            if group + 1 < GROUPS:
                transforms(group + 1, i)
            transform(table_ref, mixes[group], group, in_ref, 0, tokens, i)
            backward_products(grads[group], taps[group], mixed_ref, group, row, 0, 2 * tiles)

        each_step(tiles, step)
    for upper in (True, False):
        first_block, last_block = (tiles, 2 * tiles) if upper else (0, tiles)
        for group in range(GROUPS):

            def step(i, group=group, upper=upper, first_block=first_block, last_block=last_block):
                row = i * ROWS
                if i == 0 and upper:
                    restore(back_ref, mixed_ref, out_ref, 0, tokens, scale, group)
                    send(0, 0, group)
                if i == 0 and not upper and group < tiles // 2:
                    restore(back_ref, dtaps_ref, out_ref, tokens, tokens, scale, tiles // 2 + group)
                    send(tokens, 1, tiles // 2 + group)
                backward_products(
                    grads[group], mixes[group], dtaps_ref, group, row, first_block, last_block
                )

            each_step(tiles, step)
    for tile in range(tiles // 2):
        restore(back_ref, dtaps_ref, out_ref, tokens, tokens, scale, tile)
        send(tokens, 1, tile)
    for copy in copies:
        copy.wait()


def convolve(received, tables, scale):
    pieces, rows, _ = received.shape
    tokens = rows // 2
    freq, block = tables[0].shape
    wide = pieces * tokens // block * LANES

    def kernel(*refs):
        forward_kernel(scale, *refs)

    return pl.pallas_call(
        kernel,
        in_specs=whole(3),
        out_specs=pl.BlockSpec(memory_space=pltpu.VMEM),
        out_shape=jax.ShapeDtypeStruct((pieces, tokens, LANES), jnp.bfloat16),
        scratch_shapes=[pltpu.VMEM((freq, wide), jnp.bfloat16)]
        + [pltpu.VMEM((freq // GROUPS, wide), jnp.float32)] * (2 * GROUPS),
        name="forward",
        **params(6 * freq * block * wide, 8 * freq * wide),
    )(received, *tables)


def correlate(grads, received, tables, scale):
    pieces, tokens, _ = grads.shape
    freq, block = tables[0].shape
    wide = pieces * tokens // block * LANES

    def kernel(*refs):
        backward_kernel(scale, *refs)

    return pl.pallas_call(
        kernel,
        in_specs=whole(4),
        out_specs=pl.BlockSpec(memory_space=pltpu.HBM),
        out_shape=jax.ShapeDtypeStruct((pieces, 2 * tokens, LANES), jnp.bfloat16),
        scratch_shapes=[
            pltpu.VMEM((pieces, 2 * tokens, LANES), jnp.bfloat16),
            pltpu.SemaphoreType.DMA((2, GROUPS)),
        ]
        + [pltpu.VMEM((freq, wide), jnp.bfloat16)] * 2
        + [pltpu.VMEM((freq // GROUPS, wide), jnp.float32)] * (3 * GROUPS),
        name="backward",
        **params(10 * freq * block * wide, 8 * freq * wide),
    )(grads, received, *tables)


def sums_kernel(query_ref, up_ref, conv_ref, out_ref):
    tokens = query_ref.shape[0]
    square = jnp.zeros((tokens, LANES), jnp.float32)
    cross = jnp.zeros((tokens, LANES), jnp.float32)
    for piece in range(conv_ref.shape[0]):
        cols = slice(piece * LANES, (piece + 1) * LANES)
        gated = query_ref[:, cols].astype(jnp.float32) * conv_ref[piece].astype(jnp.float32)
        square += gated * gated
        cross += up_ref[:, cols].astype(jnp.float32) * gated
    out_ref[0:1, :] = jnp.sum(square.T, axis=0, keepdims=True)
    out_ref[1:2, :] = jnp.sum(cross.T, axis=0, keepdims=True)


def token_sums(query, upstream, conv):
    tokens, width = query.shape
    return pl.pallas_call(
        sums_kernel,
        in_specs=whole(3),
        out_specs=pl.BlockSpec(memory_space=pltpu.VMEM),
        out_shape=jax.ShapeDtypeStruct((2, tokens), jnp.float32),
        name="sums",
        **params(5 * tokens * width, 6 * tokens * width),
    )(query, upstream, conv)


def columns_of(channels, own_ref, other_ref, tokens):
    sums = (own_ref[...] + other_ref[...]) / channels
    inverse_row = lax.rsqrt(sums[0:1, :] + 1e-05)
    slope_row = inverse_row * inverse_row * inverse_row * sums[1:2, :]
    inverse = jnp.broadcast_to(inverse_row, (LANES, tokens)).T
    slope = jnp.broadcast_to(slope_row, (LANES, tokens)).T
    return inverse, slope


def grad_kernel(channels, own_ref, other_ref, query_ref, up_ref, conv_ref, grad_ref):
    inverse, slope = columns_of(channels, own_ref, other_ref, query_ref.shape[0])
    for piece in range(conv_ref.shape[0]):
        cols = slice(piece * LANES, (piece + 1) * LANES)
        query = query_ref[:, cols].astype(jnp.float32)
        gated = query * conv_ref[piece].astype(jnp.float32)
        dgated = inverse * up_ref[:, cols].astype(jnp.float32) - slope * gated
        grad_ref[piece] = (dgated * query).astype(jnp.bfloat16)


def norm_kernel(channels, own_ref, other_ref, query_ref, up_ref, conv_ref, mixer_ref, dquery_ref):
    inverse, slope = columns_of(channels, own_ref, other_ref, query_ref.shape[0])
    for piece in range(conv_ref.shape[0]):
        cols = slice(piece * LANES, (piece + 1) * LANES)
        conv = conv_ref[piece].astype(jnp.float32)
        gated = query_ref[:, cols].astype(jnp.float32) * conv
        mixer_ref[:, cols] = (gated * inverse).astype(jnp.bfloat16)
        dgated = inverse * up_ref[:, cols].astype(jnp.float32) - slope * gated
        dquery_ref[:, cols] = (dgated * conv).astype(jnp.bfloat16)


def gate_grad(own, other, query, upstream, conv, channels):
    tokens, width = query.shape

    def kernel(*refs):
        grad_kernel(channels, *refs)

    return pl.pallas_call(
        kernel,
        in_specs=whole(5),
        out_specs=pl.BlockSpec(memory_space=pltpu.VMEM),
        out_shape=jax.ShapeDtypeStruct(conv.shape, jnp.bfloat16),
        name="gate_grad",
        **params(5 * tokens * width, 8 * tokens * width),
    )(own, other, query, upstream, conv)


def gate_norm(own, other, query, upstream, conv, channels):
    tokens, width = query.shape
    step = tokens // 4

    def kernel(own_ref, other_ref, query_ref, up_ref, conv_ref, mixer_ref, dquery_ref, inv_ref, slope_ref):
        i = pl.program_id(0)

        @pl.when(i == 0)
        def _():
            inverse, slope = columns_of(channels, own_ref, other_ref, tokens)
            inv_ref[...] = inverse
            slope_ref[...] = slope

        rows = pl.ds(pl.multiple_of(i * step, step), step)
        inverse, slope = inv_ref[rows, :], slope_ref[rows, :]
        for piece in range(conv_ref.shape[0]):
            cols = slice(piece * LANES, (piece + 1) * LANES)
            conv = conv_ref[piece].astype(jnp.float32)
            gated = query_ref[:, cols].astype(jnp.float32) * conv
            mixer_ref[:, cols] = (gated * inverse).astype(jnp.bfloat16)
            dgated = inverse * up_ref[:, cols].astype(jnp.float32) - slope * gated
            dquery_ref[:, cols] = (dgated * conv).astype(jnp.bfloat16)

    flat = jax.ShapeDtypeStruct((tokens, width), jnp.bfloat16)
    wide = pl.BlockSpec((step, width), lambda i: (i, 0))
    small = pl.BlockSpec((2, tokens), lambda i: (0, 0))
    return pl.pallas_call(
        kernel,
        grid=(4,),
        in_specs=[small, small, wide, wide, pl.BlockSpec((conv.shape[0], step, LANES), lambda i: (0, i, 0))],
        out_specs=[wide, wide],
        out_shape=(flat, flat),
        scratch_shapes=[pltpu.VMEM((tokens, LANES), jnp.float32)] * 2,
        name="norm",
        **params(6 * tokens * width, 10 * tokens * width, 60),
    )(own, other, query, upstream, conv)


def unpack_kernel(
    back_ref, key_ref, value_ref, dkey_hbm, dvalue_hbm, dtaps_hbm, dkey_ref, dvalue_ref, row_sems, tap_sems
):
    tokens = key_ref.shape[0]
    step = tokens // STEPS
    rows = [slice(i * step, (i + 1) * step) for i in range(STEPS)]
    cols = [slice(i * LANES, (i + 1) * LANES) for i in range(back_ref.shape[0])]
    copies = started(
        [
            pltpu.make_async_copy(
                back_ref.at[piece, pl.ds(tokens, tokens)], dtaps_hbm.at[:, col], tap_sems.at[piece]
            )
            for piece, col in enumerate(cols)
        ]
    )
    for i, row in enumerate(rows):
        for piece, col in enumerate(cols):
            dmixed = back_ref[piece, row, :].astype(jnp.float32)
            dkey_ref[row, col] = (dmixed * value_ref[row, col].astype(jnp.float32)).astype(jnp.bfloat16)
            dvalue_ref[row, col] = (dmixed * key_ref[row, col].astype(jnp.float32)).astype(jnp.bfloat16)
        copies += started(
            [
                pltpu.make_async_copy(source.at[row], target.at[row], row_sems.at[which, i])
                for which, (source, target) in enumerate(((dkey_ref, dkey_hbm), (dvalue_ref, dvalue_hbm)))
            ]
        )
    for copy in copies:
        copy.wait()


def unpack(back, key_proj, value_proj):
    tokens, width = key_proj.shape
    flat = jax.ShapeDtypeStruct((tokens, width), jnp.bfloat16)
    return pl.pallas_call(
        unpack_kernel,
        in_specs=whole(3),
        out_specs=[pl.BlockSpec(memory_space=pltpu.HBM)] * 3,
        out_shape=(flat, flat, flat),
        scratch_shapes=[
            pltpu.VMEM((tokens, width), jnp.bfloat16),
            pltpu.VMEM((tokens, width), jnp.bfloat16),
            pltpu.SemaphoreType.DMA((2, STEPS)),
            pltpu.SemaphoreType.DMA((width // LANES,)),
        ],
        name="unpack",
        **params(2 * tokens * width, 14 * tokens * width),
    )(back, key_proj, value_proj)


def exchange(pieces):
    return lax.all_to_all(pieces, "ctx", split_axis=0, concat_axis=0, tiled=True)


def per_device_kernels(query, key_proj, value_proj, filter_taps, grad_out):
    length = query.shape[0] * lax.axis_size("ctx")
    width = query.shape[1] * lax.axis_size("tp")
    block = 2 * query.shape[0]
    scale = 1.0 / (math.sqrt(length) * block)
    tables = odd_tables(block)
    received = exchange(pack(key_proj, value_proj, filter_taps))
    conv = exchange(convolve(received, tables, scale))
    own = token_sums(query, grad_out, conv)
    other = lax.ppermute(own, "tp", [(0, 1), (1, 0)])
    grads = exchange(gate_grad(own, other, query, grad_out, conv, width))
    mixer_out, dquery = gate_norm(own, other, query, grad_out, conv, width)
    back = exchange(correlate(grads, received, tables, scale))
    dkey, dvalue, dtaps = unpack(back, key_proj, value_proj)
    return (mixer_out, dquery, dkey, dvalue, dtaps)


def per_device(query, key_proj, value_proj, filter_taps, grad_out):
    tokens, width = query.shape
    ring = lax.axis_size("ctx")
    pairs = lax.axis_size("tp") == 2
    if pairs and width == ring * LANES and tokens == LANES and ring == 4 * GROUPS:
        return per_device_kernels(query, key_proj, value_proj, filter_taps, grad_out)
    return per_device_plain(query, key_proj, value_proj, filter_taps, grad_out)


def solution(mesh):
    in_specs = (P("ctx", "tp"), P("ctx", "tp"), P("ctx", "tp"), P("ctx", "tp"), P("ctx", "tp"))
    out_specs = (P("ctx", "tp"), P("ctx", "tp"), P("ctx", "tp"), P("ctx", "tp"), P("ctx", "tp"))
    return jax.shard_map(
        per_device, mesh=mesh, in_specs=in_specs, out_specs=out_specs, check_vma=False
    )
```
